32 devices in a mesh: blk: 16 (over z, y, core), freq: 2 (over x).
Axes of the slice: x: 2, y: 2, z: 4, core: 2. Of those that a mesh axis runs over, the one named last changes fastest.
Arguments:
- forcing_hat: bfloat16 [2, 64, 2, 5, 1024, 128], P(None, 'freq', None, None, 'blk'), may hold values from -6 to 6
- mean_speed: float32 [1024, 128], P('blk'), may hold values from 0.2 to 0.9
- block_order: int32 [64], P('blk'), may hold values from 0 to 3, as said below
- block_flips: int32 [64], P('blk'), may hold values from 0 to 1
Outputs:
- response_hat: float32 [2, 64, 2, 5, 1024, 128], P(None, 'freq', None, None, 'blk')
The draws below stay inside these ranges and needn't reach their ends.
Inputs may be any that keep to these rules, and one draw needn't show every extreme that they name: `block_order`: each aligned group of 4 entries (the blocks of one index of blk) is a permutation of 0 to 3.
All inputs are finite; a program needn't handle non-finite values.
Results may differ from the reference program's by a relative error of at most 0.0021.
Values sent between devices are 32-bit elements; how exact they have to be, the bound alone decides.
A program may use at most 64 MiB of HBM per device.

```python
import math
import jax
import jax.numpy as jnp
from jax import lax

NJ = 128
BPD = 4
K = 2
F = 64
STEPS = 8
NBLOCKS = 64
ROWS = 1024


def draw_block_order(key, part):
    scores = jax.random.randint(key, (NBLOCKS // BPD, BPD), 0, 1 << 16) * BPD + jnp.arange(BPD, dtype=jnp.int32)[None, :]
    return jnp.argsort(scores, axis=1, stable=True).astype(jnp.int32).reshape(NBLOCKS)


def set_ends(drawn, own_key, low, high):
    dims = drawn.shape
    index_at = [jax.random.randint(jax.random.fold_in(own_key, axis), (), 0, dims[axis]) for axis in range(len(dims))]
    drawn = drawn.at[tuple(index_at)].set(low)
    longest = dims.index(max(dims))
    index_at[longest] = (index_at[longest] + 1) % dims[longest]
    return drawn.at[tuple(index_at)].set(high)


def level_of(rng, shape, pieces, smallest, largest):
    def one(dim, blocks):
        heights = jax.random.uniform(jax.random.fold_in(jax.random.fold_in(rng, 6), dim), (blocks,), jnp.float32, smallest / len(pieces), largest / len(pieces))
        return jnp.repeat(jnp.exp(heights), shape[dim] // blocks).reshape((-1,) + (1,) * (len(shape) - dim - 1))

    gain = one(*pieces[0])
    for cut in pieces[1:]:
        gain = gain * one(*cut)
    return gain


def normal_values(key, shape, spread, limit, shards=(), held_as=jnp.bfloat16):
    gain = level_of(key, shape, shards, -0.22, 0.18) if shards else 1.0
    array = jax.random.normal(key, shape, jnp.float32) * spread * gain
    return jnp.minimum(jnp.maximum(array, -limit), limit).astype(held_as)


def setup_inputs(seed: int = 0) -> dict:
    arg_keys = jax.random.split(jax.random.key(seed), 5)
    forcing_hat = normal_values(arg_keys[0], (2, F, K, 5, ROWS, NJ), 1.0, 6.0, ((1, 2), (4, 16)))
    mean_speed = jnp.clip(0.2 + 0.7 * jax.random.uniform(arg_keys[1], (ROWS, NJ), jnp.float32) ** level_of(arg_keys[1], (ROWS, NJ), ((0, 16),), -0.2, 0.2), 0.2, 0.9)
    block_order = draw_block_order(jax.random.fold_in(arg_keys[4], 71), 0)
    block_flips = set_ends(jax.random.randint(arg_keys[3], (NBLOCKS,), 0, 2), jax.random.fold_in(arg_keys[3], 1), 0, 1).astype(jnp.int32)
    return {"forcing_hat": forcing_hat, "mean_speed": mean_speed, "block_order": block_order, "block_flips": block_flips}


time_step = 0.4
viscosity = 0.5

def flip_blocks(blocked, flip_flags):
    return jnp.where((flip_flags == 1)[:, None, None], blocked[..., ::-1], blocked)

def to_chain(values, chain_ids, flip_flags, block_count):
    blocked = values.reshape(values.shape[:-2] + (block_count, values.shape[-2] // block_count, values.shape[-1]))
    placed = jnp.take(blocked, chain_ids, axis=-3)
    placed = flip_blocks(placed, jnp.take(flip_flags, chain_ids))
    return placed.reshape(values.shape)

def from_chain(values, chain_ids, flip_flags, block_count):
    inverse = jnp.argsort(chain_ids).astype(jnp.int32)
    blocked = values.reshape(values.shape[:-2] + (block_count, values.shape[-2] // block_count, values.shape[-1]))
    placed = jnp.take(blocked, inverse, axis=-3)
    placed = flip_blocks(placed, flip_flags)
    return placed.reshape(values.shape)

def tendency(extended, mean_speed):
    center = extended[:, :, 1:-1, 1:-1]
    upper_row = extended[:, :, 2:, 1:-1]
    lower_row = extended[:, :, :-2, 1:-1]
    right_col = extended[:, :, 1:-1, 2:]
    left_col = extended[:, :, 1:-1, :-2]
    stream_diff = 0.5 * (upper_row - lower_row)
    cross_diff = 0.5 * (right_col - left_col)
    laplace = upper_row + lower_row + right_col + left_col - 4.0 * center
    advection = -mean_speed * stream_diff
    divergence = stream_diff[:, 1] + cross_diff[:, 2]
    rates = jnp.stack([advection[:, 0] - divergence, advection[:, 1] - stream_diff[:, 3], advection[:, 2] - cross_diff[:, 3], advection[:, 3] - divergence, advection[:, 4]], axis=1)
    return rates + viscosity * laplace

def synthesis_table(freq_ids):
    angular = (freq_ids + 1.0) * (math.pi / F)
    times = jnp.arange(STEPS, dtype=jnp.float32)
    phase = times[:, None] * angular[None, :]
    table = jnp.stack([jnp.cos(phase), -jnp.sin(phase)], axis=1) / math.sqrt(F)
    return table.astype(jnp.bfloat16)

def analysis_table(freq_ids):
    angular = (freq_ids + 1.0) * (math.pi / F)
    times = jnp.arange(1, STEPS + 1, dtype=jnp.float32)
    phase = angular[:, None] * times[None, :]
    return jnp.stack([jnp.cos(phase), -jnp.sin(phase)], axis=0) / math.sqrt(STEPS)

def reference(forcing_hat, mean_speed, block_order, block_flips):
    chain_ids = (jnp.arange(NBLOCKS, dtype=jnp.int32) // BPD * BPD + block_order).astype(jnp.int32)
    freq_ids = jnp.arange(F, dtype=jnp.float32)
    synth = synthesis_table(freq_ids).astype(jnp.float32)
    forcing = jnp.stack([jnp.einsum('scm,cmvrj->svrj', synth, forcing_hat[:, :, vector].astype(jnp.float32), precision=lax.Precision.HIGHEST) for vector in range(K)], axis=0)
    forcing = to_chain(forcing, chain_ids, block_flips, NBLOCKS)
    speed_chain = to_chain(mean_speed, chain_ids, block_flips, NBLOCKS)
    fields_now = jnp.zeros((K, 5, ROWS, NJ), jnp.float32)
    history = []
    for step_index in range(STEPS):
        extended = jnp.pad(fields_now, ((0, 0), (0, 0), (1, 1), (1, 1)))
        fields_now = fields_now + time_step * (tendency(extended, speed_chain) + forcing[:, step_index])
        history.append(fields_now)
    history = from_chain(jnp.stack(history, axis=1), chain_ids, block_flips, NBLOCKS)
    analysis = analysis_table(freq_ids)
    return jnp.stack([jnp.einsum('cms,svrj->cmvrj', analysis, history[vector], precision=lax.Precision.HIGHEST) for vector in range(K)], axis=2)
```

```python
import functools
import math

import jax
import jax.numpy as jnp
import numpy as np
from jax import lax
from jax.experimental import pallas as pl
from jax.experimental.pallas import tpu as pltpu
from jax.sharding import PartitionSpec as P

STEPS = 8
HALO = 8
DT = 0.4
NU = 0.5


def synthesis_weights(total, shards, rows):
    omega = (np.arange(total, dtype=np.float64) + 1.0) * (math.pi / total)
    phase = np.arange(STEPS)[:, None] * omega[None, :]
    table = np.stack([np.cos(phase), -np.sin(phase)], axis=1) / math.sqrt(total)
    table = table.astype(np.float32).astype(jnp.bfloat16).astype(np.float32)
    local = total // shards
    eye = np.eye(rows, dtype=np.float32)
    out = []
    for i in range(shards):
        part = table[:, :, i * local : (i + 1) * local].reshape(STEPS, 2 * local)
        out.append(np.kron(part, eye))
    return np.stack(out).astype(jnp.bfloat16)


def analysis_weights(total, shards, rows):
    omega = (np.arange(total, dtype=np.float64) + 1.0) * (math.pi / total)
    phase = omega[:, None] * np.arange(1, STEPS + 1)[None, :]
    table = np.stack([np.cos(phase), -np.sin(phase)], axis=0) / math.sqrt(STEPS)
    table = table.astype(np.float32)
    high = table.astype(jnp.bfloat16).astype(np.float32)
    low = table - high
    local = total // shards
    eye = np.eye(rows, dtype=np.float32)
    out = []
    for i in range(shards):
        cut = slice(i * local, (i + 1) * local)
        hi = np.kron(high[:, cut].reshape(2 * local, STEPS), eye)
        lo = np.kron(low[:, cut].reshape(2 * local, STEPS), eye)
        out.append(np.concatenate([hi, hi, lo], axis=1))
    return np.stack(out).astype(jnp.bfloat16)


def lane_map(flag, rows, cols):
    lane = lax.broadcasted_iota(jnp.int32, (rows, cols), 1)
    return jnp.where(flag == 1, cols - 1 - lane, lane)


def reorder_lanes(x, flag):
    index = lane_map(flag, *x.shape)
    return jnp.take_along_axis(x, index, axis=1, mode="promise_in_bounds")


def synth_kernel(blocks, order, flips, shard, x_ref, w_ref, speed_ref, early_ref, late_ref, chain_ref):
    rows = x_ref.shape[4] // blocks
    cols = x_ref.shape[5]
    depth = x_ref.shape[0] * x_ref.shape[1] * rows
    weights = w_ref[0]
    for pair in range(0, blocks, 2):
        cut = []
        for p in (pair, pair + 1):
            start = pl.multiple_of(order[p] * rows, rows)
            cut.append(x_ref[:, :, 0, 0, pl.ds(start, rows), :].reshape(depth, cols))
        made = jnp.dot(weights, jnp.concatenate(cut, axis=1), preferred_element_type=jnp.float32)
        for i, p in enumerate((pair, pair + 1)):
            part = reorder_lanes(made[:, i * cols : (i + 1) * cols], flips[order[p]])
            part = part.reshape(STEPS, rows, cols)
            early_ref[:, 0, p * rows : (p + 1) * rows, :] = part[: STEPS - 1]
            late_ref[0, p * rows : (p + 1) * rows, :] = part[STEPS - 1]

    @pl.when(pl.program_id(0) == 0)
    def _():
        for p in range(blocks):
            start = pl.multiple_of(order[p] * rows, rows)
            part = speed_ref[pl.ds(start, rows), :]
            chain_ref[p * rows : (p + 1) * rows, :] = reorder_lanes(part, flips[order[p]])


def synthesize(k, forcing_hat, weights, speed, order, flips, shard):
    parts, local, _, fields, rows, cols = forcing_hat.shape
    blocks = order.shape[0]
    return pl.pallas_call(
        functools.partial(synth_kernel, blocks),
        out_shape=(
            jax.ShapeDtypeStruct((STEPS - 1, fields, rows, cols), jnp.float32),
            jax.ShapeDtypeStruct((fields, rows, cols), jnp.float32),
            jax.ShapeDtypeStruct((rows, cols), jnp.float32),
        ),
        grid_spec=pltpu.PrefetchScalarGridSpec(
            num_scalar_prefetch=3,
            grid=(fields,),
            in_specs=[
                pl.BlockSpec((parts, local, 1, 1, rows, cols), lambda v, *_: (0, 0, k, v, 0, 0)),
                pl.BlockSpec((1,) + weights.shape[1:], lambda v, o, f, s: (s[0], 0, 0)),
                pl.BlockSpec((rows, cols), lambda v, *_: (0, 0)),
            ],
            out_specs=(
                pl.BlockSpec((STEPS - 1, 1, rows, cols), lambda v, *_: (0, v, 0, 0)),
                pl.BlockSpec((1, rows, cols), lambda v, *_: (v, 0, 0)),
                pl.BlockSpec((rows, cols), lambda v, *_: (0, 0)),
            ),
        ),
        cost_estimate=pl.CostEstimate(flops=10**9, bytes_accessed=8 * 10**6, transcendentals=0),
        name=f"synth{k}",
    )(order, flips, shard, forcing_hat, weights, speed)


def advance(window, speed, forced):
    def around(v):
        center, upper, lower = window(v)
        cols = center.shape[1]
        lane = lax.broadcasted_iota(jnp.int32, center.shape, 1)
        right = jnp.where(lane == cols - 1, 0.0, pltpu.roll(center, cols - 1, 1))
        left = jnp.where(lane == 0, 0.0, pltpu.roll(center, 1, 1))
        stream = 0.5 * (upper - lower)
        cross = 0.5 * (right - left)
        spread = NU * (upper + lower + right + left - 4.0 * center)
        return center, stream, cross, spread

    def close(v, parts, rate):
        center, stream, _, spread = parts
        return center + DT * (rate - speed * stream + spread + forced(v))

    u = around(1)
    w = around(2)
    pressure = around(3)
    divergence = u[1] + w[2]
    new_u = close(1, u, -pressure[1])
    new_w = close(2, w, -pressure[2])
    new_p = close(3, pressure, -divergence)
    new_rho = close(0, around(0), -divergence)
    new_s = close(4, around(4), 0.0)
    return [new_rho, new_u, new_w, new_p, new_s]


def march_kernel(count, place, *refs):
    terms = refs[:count]
    before_ref, after_ref, speed_ref, past_ref, state = refs[count:]
    rows = terms[0].shape[2]
    span = rows + 2 * HALO
    fields = state.shape[1]
    state[...] = jnp.zeros_like(state)
    speed = speed_ref[...]
    row = lax.broadcasted_iota(jnp.int32, speed.shape, 0)
    low = jnp.where(place[0] == 0, HALO, 0)
    high = jnp.where(place[0] == place[1] - 1, span - HALO, span)
    inside = (row >= low) & (row < high)

    def step(n, carry):
        now = lax.rem(n, 2)

        def window(v):
            return tuple(state[now, v, pl.ds(HALO + d, span), :] for d in (0, 1, -1))

        def forced(v):
            own = terms[0][n, v]
            for term in terms[1:]:
                own = own + term[n, v]
            return jnp.concatenate([before_ref[n, v], own, after_ref[n, v]], axis=0)

        for v, new in enumerate(advance(window, speed, forced)):
            new = jnp.where(inside, new, 0.0)
            state[1 - now, v, pl.ds(HALO, span), :] = new
            past_ref[n, v] = new
        return carry

    lax.fori_loop(0, STEPS - 1, step, 0)


def march(k, terms, before, after, speed, place):
    steps, fields, rows, cols = terms[0].shape
    span = rows + 2 * HALO
    vmem = pl.BlockSpec(memory_space=pltpu.VMEM)
    return pl.pallas_call(
        functools.partial(march_kernel, len(terms)),
        out_shape=jax.ShapeDtypeStruct((steps, fields, span, cols), jnp.float32),
        in_specs=[pl.BlockSpec(memory_space=pltpu.SMEM)] + [vmem] * (len(terms) + 3),
        out_specs=vmem,
        scratch_shapes=[pltpu.VMEM((2, fields, span + 2 * HALO, cols), jnp.float32)],
        cost_estimate=pl.CostEstimate(flops=10**8, bytes_accessed=4 * 10**6, transcendentals=0),
        name=f"march{k}",
    )(place, *terms, before, after, speed)


def finish_kernel(blocks, count, order, flips, shard, past_ref, *refs):
    terms = refs[:count]
    speed_ref, w_ref = refs[count : count + 2]
    out_ref, last = refs[-2:]
    fields, rows, cols = last.shape
    v = pl.program_id(0)

    @pl.when(v == 0)
    def _():
        def window(f):
            return tuple(past_ref[STEPS - 2, f, pl.ds(HALO + d, rows), :] for d in (0, 1, -1))

        def forced(f):
            own = terms[0][f]
            for term in terms[1:]:
                own = own + term[f]
            return own

        for f, new in enumerate(advance(window, speed_ref[HALO : HALO + rows, :], forced)):
            last[f] = new

    weights = w_ref[0]
    size = rows // blocks
    for b in range(blocks):
        where = jnp.int32(0)
        for p in range(1, blocks):
            where = jnp.where(order[p] == b, p, where)
        columns = []
        for h in range(0, size, HALO):
            start = pl.multiple_of(where * size + h, HALO)
            x = jnp.concatenate(
                [past_ref[:, v, pl.ds(start + HALO, HALO), :], last[v, pl.ds(start, HALO), :][None]], axis=0
            ).reshape(STEPS * HALO, cols)
            x = reorder_lanes(x, flips[b])
            hi = x.astype(jnp.bfloat16)
            lo = (x - hi.astype(jnp.float32)).astype(jnp.bfloat16)
            columns.append(jnp.concatenate([hi, lo, hi], axis=0))
        made = jnp.dot(weights, jnp.concatenate(columns, axis=1), preferred_element_type=jnp.float32)
        for i, h in enumerate(range(0, size, HALO)):
            part = made[:, i * cols : (i + 1) * cols]
            part = part.reshape(out_ref.shape[0], out_ref.shape[1], HALO, cols)
            out_ref[:, :, 0, 0, b * size + h : b * size + h + HALO, :] = part


def finish(k, shape, past, terms, speed, weights, order, flips, shard, partial):
    parts, local, _, fields, rows, cols = shape
    blocks = order.shape[0]

    def whole(x):
        return pl.BlockSpec(x.shape, lambda v, *_: (0,) * x.ndim)

    operands = [order, flips, shard, past, *terms, speed, weights]
    specs = [whole(x) for x in (past, *terms, speed)]
    specs.append(pl.BlockSpec((1,) + weights.shape[1:], lambda v, o, f, s: (s[0], 0, 0)))
    aliases = {}
    if partial is not None:
        aliases = {len(operands): 0}
        operands.append(partial)
        specs.append(pl.BlockSpec(memory_space=pl.ANY))
    return pl.pallas_call(
        functools.partial(finish_kernel, blocks, len(terms)),
        out_shape=jax.ShapeDtypeStruct(shape, jnp.float32),
        grid_spec=pltpu.PrefetchScalarGridSpec(
            num_scalar_prefetch=3,
            grid=(fields,),
            in_specs=specs,
            out_specs=pl.BlockSpec((parts, local, 1, 1, rows, cols), lambda v, *_: (0, 0, k, v, 0, 0)),
            scratch_shapes=[pltpu.VMEM((fields, rows, cols), jnp.float32)],
        ),
        input_output_aliases=aliases,
        cost_estimate=pl.CostEstimate(flops=10**9, bytes_accessed=12 * 10**6, transcendentals=0),
        name=f"finish{k}",
    )(*operands)


def shared(x):
    peers = lax.axis_size("freq")
    if peers == 2:
        return [x, lax.ppermute(x, "freq", [(0, 1), (1, 0)])]
    return [lax.psum(x, "freq")]


def halos(x, dim):
    peers = lax.axis_size("blk")
    up = [(i, i + 1) for i in range(peers - 1)]
    down = [(j, i) for i, j in up]
    length = x[0].shape[dim]
    tail = sum(lax.slice_in_dim(y, length - HALO, length, axis=dim) for y in x)
    head = sum(lax.slice_in_dim(y, 0, HALO, axis=dim) for y in x)
    return lax.ppermute(tail, "blk", up), lax.ppermute(head, "blk", down)


def local(forcing_hat, mean_speed, block_order, block_flips):
    peers = lax.axis_size("freq")
    total = forcing_hat.shape[1] * peers
    vectors = forcing_hat.shape[2]
    size = forcing_hat.shape[4] // block_order.shape[0]
    shard = lax.axis_index("freq").astype(jnp.int32).reshape(1)
    place = jnp.stack([lax.axis_index("blk"), lax.axis_size("blk")]).astype(jnp.int32)
    synth = jnp.asarray(synthesis_weights(total, peers, size))
    analysis = jnp.asarray(analysis_weights(total, peers, HALO))
    made = [
        synthesize(k, forcing_hat, synth, mean_speed, block_order, block_flips, shard) for k in range(vectors)
    ]
    chain = made[0][2]
    above, below = halos([chain], 0)
    speed = jnp.concatenate([above, chain, below], axis=0)
    shape = forcing_hat.shape
    early = [shared(m[0]) for m in made]
    late = [shared(m[1]) for m in made]
    out = None
    for k in range(vectors):
        before, after = halos(early[k], 2)
        past = march(k, early[k], before, after, speed, place)
        out = finish(k, shape, past, late[k], speed, analysis, block_order, block_flips, shard, out)
    return out


def solution(mesh):
    placed = (P(None, "freq", None, None, "blk", None), P("blk", None), P("blk"), P("blk"))
    return jax.shard_map(
        local,
        mesh=mesh,
        in_specs=placed,
        out_specs=P(None, "freq", None, None, "blk", None),
        check_vma=False,
    )
```

```python
import functools
import math

import jax
import jax.numpy as jnp
import numpy as np
from jax import lax
from jax.experimental import pallas as pl
from jax.experimental.pallas import tpu as pltpu
from jax.sharding import PartitionSpec as P

STEPS = 8
HALO = 8
DT = 0.4
NU = 0.5


def synthesis_weights(total, shards, rows):
    omega = (np.arange(total, dtype=np.float64) + 1.0) * (math.pi / total)
    phase = np.arange(STEPS)[:, None] * omega[None, :]
    table = np.stack([np.cos(phase), -np.sin(phase)], axis=1) / math.sqrt(total)
    table = table.astype(np.float32).astype(jnp.bfloat16).astype(np.float32)
    local = total // shards
    eye = np.eye(rows, dtype=np.float32)
    out = []
    for i in range(shards):
        part = table[:, :, i * local : (i + 1) * local].reshape(STEPS, 2 * local)
        out.append(np.kron(part, eye))
    return np.stack(out).astype(jnp.bfloat16)


def analysis_weights(total, shards, rows):
    omega = (np.arange(total, dtype=np.float64) + 1.0) * (math.pi / total)
    phase = omega[:, None] * np.arange(1, STEPS + 1)[None, :]
    table = np.stack([np.cos(phase), -np.sin(phase)], axis=0) / math.sqrt(STEPS)
    table = table.astype(np.float32)
    high = table.astype(jnp.bfloat16).astype(np.float32)
    low = table - high
    local = total // shards
    eye = np.eye(rows, dtype=np.float32)
    out = []
    for i in range(shards):
        cut = slice(i * local, (i + 1) * local)
        hi = np.kron(high[:, cut].reshape(2 * local, STEPS), eye)
        lo = np.kron(low[:, cut].reshape(2 * local, STEPS), eye)
        out.append(np.concatenate([hi, hi, lo], axis=1))
    return np.stack(out).astype(jnp.bfloat16)


def lane_map(flag, rows, cols):
    lane = lax.broadcasted_iota(jnp.int32, (rows, cols), 1)
    return jnp.where(flag == 1, cols - 1 - lane, lane)


def reorder_lanes(x, flag):
    index = lane_map(flag, *x.shape)
    return jnp.take_along_axis(x, index, axis=1, mode="promise_in_bounds")


def synth_kernel(blocks, cuts, waits, order, flips, shard, x_ref, w_ref, *refs):
    rows = x_ref.shape[4] // blocks
    cols = x_ref.shape[5]
    depth = x_ref.shape[0] * x_ref.shape[1] * rows
    outs = refs[waits:]
    weights = w_ref[0]
    for pair in range(0, blocks, 2):
        cut = []
        for p in (pair, pair + 1):
            start = pl.multiple_of(order[p] * rows, rows)
            cut.append(x_ref[:, :, 0, 0, pl.ds(start, rows), :].reshape(depth, cols))
        made = jnp.dot(weights, jnp.concatenate(cut, axis=1), preferred_element_type=jnp.float32)
        for i, p in enumerate((pair, pair + 1)):
            part = reorder_lanes(made[:, i * cols : (i + 1) * cols], flips[order[p]])
            part = part.reshape(STEPS, rows, cols)
            for (low, high), out in zip(cuts, outs):
                out[:, 0, p * rows : (p + 1) * rows, :] = part[low:high]


def spread_of(group):
    return group[0], (group[1] - group[0] if len(group) > 1 else 1)


def synthesize(k, group, cuts, forcing_hat, weights, order, flips, shard, after):
    parts, local, _, _, rows, cols = forcing_hat.shape
    blocks = order.shape[0]
    first, stride = spread_of(group)
    many = len(group)
    return pl.pallas_call(
        functools.partial(synth_kernel, blocks, cuts, len(after)),
        out_shape=[jax.ShapeDtypeStruct((high - low, many, rows, cols), jnp.float32) for low, high in cuts],
        grid_spec=pltpu.PrefetchScalarGridSpec(
            num_scalar_prefetch=3,
            grid=(many,),
            in_specs=[
                pl.BlockSpec(
                    (parts, local, 1, 1, rows, cols), lambda g, *_: (0, 0, k, first + g * stride, 0, 0)
                ),
                pl.BlockSpec((1,) + weights.shape[1:], lambda g, o, f, s: (s[0], 0, 0)),
            ]
            + [pl.BlockSpec(memory_space=pl.ANY)] * len(after),
            out_specs=[pl.BlockSpec((high - low, 1, rows, cols), lambda g, *_: (0, g, 0, 0)) for low, high in cuts],
        ),
        cost_estimate=pl.CostEstimate(flops=10**9, bytes_accessed=2 * 10**6 * many, transcendentals=0),
        name=f"synth{k}_{first}",
    )(order, flips, shard, forcing_hat, weights, *after)


def chain_kernel(blocks, order, flips, speed_ref, chain_ref):
    rows = speed_ref.shape[0] // blocks
    for p in range(blocks):
        start = pl.multiple_of(order[p] * rows, rows)
        chain_ref[p * rows : (p + 1) * rows, :] = reorder_lanes(speed_ref[pl.ds(start, rows), :], flips[order[p]])


def chain_speed(speed, order, flips):
    smem = pl.BlockSpec(memory_space=pltpu.SMEM)
    vmem = pl.BlockSpec(memory_space=pltpu.VMEM)
    return pl.pallas_call(
        functools.partial(chain_kernel, order.shape[0]),
        out_shape=jax.ShapeDtypeStruct(speed.shape, speed.dtype),
        in_specs=[smem, smem, vmem],
        out_specs=vmem,
        name="chain_speed",
    )(order, flips, speed)


def total_of(terms, *index):
    own = terms[0][index]
    for term in terms[1:]:
        own = own + term[index]
    return own


def edge_kernel(sizes, *refs):
    tail_ref, head_ref = refs[-2:]
    at, field = 0, 0
    steps = STEPS - 1
    for count, many in sizes:
        terms = refs[at : at + count]
        rows = terms[0].shape[2]
        tail_ref[:, field : field + many] = total_of(
            terms, slice(0, steps), slice(None), slice(rows - HALO, rows), slice(None)
        )
        head_ref[:, field : field + many] = total_of(terms, slice(0, steps), slice(None), slice(0, HALO), slice(None))
        at, field = at + count, field + many


def edges(pieces, after):
    steps = STEPS - 1
    cols = pieces[0][0].shape[3]
    fields = sum(p[0].shape[1] for p in pieces)
    vmem = pl.BlockSpec(memory_space=pltpu.VMEM)
    flat = [t for p in pieces for t in p]
    shape = jax.ShapeDtypeStruct((steps, fields, HALO, cols), jnp.float32)
    return pl.pallas_call(
        functools.partial(edge_kernel, [(len(p), p[0].shape[1]) for p in pieces]),
        out_shape=(shape, shape),
        in_specs=[vmem] * len(flat) + [pl.BlockSpec(memory_space=pl.ANY)] * len(after),
        out_specs=(vmem, vmem),
        cost_estimate=pl.CostEstimate(flops=10**6, bytes_accessed=10**6, transcendentals=0),
        name="edges",
    )(*flat, *after)


def advance(group, window, speed, forced):
    held = {}

    def around(v):
        if v not in held:
            center, upper, lower = window(v)
            cols = center.shape[1]
            lane = lax.broadcasted_iota(jnp.int32, center.shape, 1)
            right = jnp.where(lane == cols - 1, 0.0, pltpu.roll(center, cols - 1, 1))
            left = jnp.where(lane == 0, 0.0, pltpu.roll(center, 1, 1))
            stream = 0.5 * (upper - lower)
            cross = 0.5 * (right - left)
            spread = NU * (upper + lower + right + left - 4.0 * center)
            held[v] = center, stream, cross, spread
        return held[v]

    def divergence():
        return around(1)[1] + around(2)[2]

    rates = {
        0: lambda: -divergence(),
        1: lambda: -around(3)[1],
        2: lambda: -around(3)[2],
        3: lambda: -divergence(),
        4: lambda: 0.0,
    }
    for v in group:
        center, stream, _, spread = around(v)
        yield center + DT * (rates[v]() - speed * stream + spread + forced(v))


def piece_of(group, sizes, refs, v):
    at, first = 0, 0
    where = group.index(v)
    for count, many in sizes:
        if where < first + many:
            return refs[at : at + count], where - first
        at, first = at + count, first + many


def march_kernel(group, sizes, carrier, place, *refs):
    used = sum(c for c, _ in sizes)
    terms, rest = refs[:used], refs[used:]
    before_ref, after_ref, speed_ref = rest[:3]
    other = rest[3] if carrier else None
    past_ref = rest[-1]
    rows = terms[0].shape[2]
    span = rows + 2 * HALO
    past_ref[0] = jnp.zeros(past_ref.shape[1:], jnp.float32)
    speed = speed_ref[...]
    row = lax.broadcasted_iota(jnp.int32, speed.shape, 0)
    low = jnp.where(place[0] == 0, HALO, 0)
    high = jnp.where(place[0] == place[1] - 1, span - HALO, span)
    inside = (row >= low) & (row < high)

    def step(n, carry):
        def window(v):
            if v in group:
                center = past_ref[n, group.index(v)]
            else:
                center = other[n, carrier.index(v)]
            return center, pltpu.roll(center, span - 1, 0), pltpu.roll(center, 1, 0)

        def forced(v):
            held, i = piece_of(group, sizes, terms, v)
            g = group.index(v)
            return jnp.concatenate([before_ref[n, g], total_of(held, n, i), after_ref[n, g]], axis=0)

        for g, new in enumerate(advance(group, window, speed, forced)):
            past_ref[n + 1, g] = jnp.where(inside, new, 0.0)
        return carry

    lax.fori_loop(0, STEPS - 1, step, 0)


def march(group, pieces, before, after, speed, place, carrier, other):
    _, _, rows, cols = pieces[0][0].shape
    span = rows + 2 * HALO
    vmem = pl.BlockSpec(memory_space=pltpu.VMEM)
    flat = [t for p in pieces for t in p]
    operands = [*flat, before, after, speed] + ([other] if carrier else [])
    return pl.pallas_call(
        functools.partial(march_kernel, group, [(len(p), p[0].shape[1]) for p in pieces], carrier),
        out_shape=jax.ShapeDtypeStruct((STEPS, len(group), span, cols), jnp.float32),
        in_specs=[pl.BlockSpec(memory_space=pltpu.SMEM)] + [vmem] * len(operands),
        out_specs=vmem,
        cost_estimate=pl.CostEstimate(flops=10**8, bytes_accessed=4 * 10**6, transcendentals=0),
        name="march",
    )(place, *operands)


def finish_kernel(blocks, group, sizes, carrier, order, flips, shard, past_ref, *refs):
    used = sum(c for c, _ in sizes)
    terms, rest = refs[:used], refs[used:]
    speed_ref, w_ref = rest[:2]
    other = rest[2] if carrier else None
    out_ref, last = refs[-2:]
    _, rows, cols = last.shape
    g = pl.program_id(0)

    @pl.when(g == 0)
    def _():
        def window(v):
            if v in group:
                source, i = past_ref, group.index(v)
            else:
                source, i = other, carrier.index(v)
            return tuple(source[STEPS - 1, i, pl.ds(HALO + d, rows), :] for d in (0, 1, -1))

        def forced(v):
            held, i = piece_of(group, sizes, terms, v)
            return total_of(held, held[0].shape[0] - 1, i)

        for i, new in enumerate(advance(group, window, speed_ref[HALO : HALO + rows, :], forced)):
            last[i] = new

    weights = w_ref[0]
    size = rows // blocks
    for b in range(blocks):
        where = jnp.int32(0)
        for p in range(1, blocks):
            where = jnp.where(order[p] == b, p, where)
        columns = []
        for h in range(0, size, HALO):
            start = pl.multiple_of(where * size + h, HALO)
            x = jnp.concatenate(
                [past_ref[1:, g, pl.ds(start + HALO, HALO), :], last[g, pl.ds(start, HALO), :][None]], axis=0
            ).reshape(STEPS * HALO, cols)
            x = reorder_lanes(x, flips[b])
            hi = x.astype(jnp.bfloat16)
            lo = (x - hi.astype(jnp.float32)).astype(jnp.bfloat16)
            columns.append(jnp.concatenate([hi, lo, hi], axis=0))
        made = jnp.dot(weights, jnp.concatenate(columns, axis=1), preferred_element_type=jnp.float32)
        for i, h in enumerate(range(0, size, HALO)):
            part = made[:, i * cols : (i + 1) * cols]
            part = part.reshape(out_ref.shape[0], out_ref.shape[1], HALO, cols)
            out_ref[:, :, 0, 0, b * size + h : b * size + h + HALO, :] = part


def finish(k, group, shape, past, pieces, speed, weights, order, flips, shard, carrier, other, partial):
    parts, local, _, _, rows, cols = shape
    blocks = order.shape[0]
    first, stride = spread_of(group)

    def whole(x):
        return pl.BlockSpec(x.shape, lambda g, *_: (0,) * x.ndim)

    flat = [t for p in pieces for t in p]
    operands = [order, flips, shard, past, *flat, speed, weights]
    specs = [whole(x) for x in (past, *flat, speed)]
    specs.append(pl.BlockSpec((1,) + weights.shape[1:], lambda g, o, f, s: (s[0], 0, 0)))
    if carrier:
        operands.append(other)
        specs.append(whole(other))
    aliases = {}
    if partial is not None:
        aliases = {len(operands): 0}
        operands.append(partial)
        specs.append(pl.BlockSpec(memory_space=pl.ANY))
    return pl.pallas_call(
        functools.partial(finish_kernel, blocks, group, [(len(p), p[0].shape[1]) for p in pieces], carrier),
        out_shape=jax.ShapeDtypeStruct(shape, jnp.float32),
        grid_spec=pltpu.PrefetchScalarGridSpec(
            num_scalar_prefetch=3,
            grid=(len(group),),
            in_specs=specs,
            out_specs=pl.BlockSpec(
                (parts, local, 1, 1, rows, cols), lambda g, *_: (0, 0, k, first + g * stride, 0, 0)
            ),
            scratch_shapes=[pltpu.VMEM((len(group), rows, cols), jnp.float32)],
        ),
        input_output_aliases=aliases,
        cost_estimate=pl.CostEstimate(flops=10**9, bytes_accessed=3 * 10**6 * len(group), transcendentals=0),
        name=f"finish{k}_{first}",
    )(*operands)


def shared(x):
    peers = lax.axis_size("freq")
    if peers == 2:
        return [x, lax.ppermute(x, "freq", [(0, 1), (1, 0)])]
    return [lax.psum(x, "freq")]


def neighbours(tail, head):
    peers = lax.axis_size("blk")
    up = [(i, i + 1) for i in range(peers - 1)]
    down = [(j, i) for i, j in up]
    return lax.ppermute(tail, "blk", up), lax.ppermute(head, "blk", down)


def plan(vectors):
    flow, passive, every = (1, 2, 3), (0, 4), (0, 1, 2, 3, 4)
    whole = ((0, STEPS),)
    jobs = []
    for k in range(vectors - 1):
        jobs.append((k, every, (((0, 1), whole), ((2, 3, 4), whole)), ()))
    k = vectors - 1
    jobs.append((k, flow, ((flow, whole),), ()))
    jobs.append((k, passive, ((passive, whole),), flow))
    return jobs


def local(forcing_hat, mean_speed, block_order, block_flips):
    peers = lax.axis_size("freq")
    total = forcing_hat.shape[1] * peers
    shape = forcing_hat.shape
    size = shape[4] // block_order.shape[0]
    shard = lax.axis_index("freq").astype(jnp.int32).reshape(1)
    place = jnp.stack([lax.axis_index("blk"), lax.axis_size("blk")]).astype(jnp.int32)
    synth = jnp.asarray(synthesis_weights(total, peers, size))
    analysis = jnp.asarray(analysis_weights(total, peers, HALO))
    jobs = plan(shape[2])
    sent, earlier = [], ()
    for k, _, parts, _ in jobs:
        pieces = []
        for part, cuts in parts:
            made = synthesize(k, part, cuts, forcing_hat, synth, block_order, block_flips, shard, earlier)
            earlier = (made[0],)
            pieces.append([shared(x) for x in made])
        sent.append(pieces)
    chain = chain_speed(mean_speed, block_order, block_flips)
    above, below = neighbours(chain[-HALO:], chain[:HALO])
    speed = jnp.concatenate([above, chain, below], axis=0)
    out = None
    history = {}
    for (k, group, _, carrier), made in zip(jobs, sent):
        early = [piece[0] for piece in made]
        late = [piece[-1] for piece in made]
        before, after = neighbours(*edges(early, () if out is None else (out,)))
        other = history.get((k, carrier))
        past = march(group, early, before, after, speed, place, carrier, other)
        history[k, group] = past
        out = finish(
            k, group, shape, past, late, speed, analysis, block_order, block_flips, shard, carrier, other, out
        )
    return out


def solution(mesh):
    placed = (P(None, "freq", None, None, "blk", None), P("blk", None), P("blk"), P("blk"))
    return jax.shard_map(
        local,
        mesh=mesh,
        in_specs=placed,
        out_specs=P(None, "freq", None, None, "blk", None),
        check_vma=False,
    )
```

```python
import functools
import math

import jax
import jax.numpy as jnp
import numpy as np
from jax import lax
from jax.experimental import pallas as pl
from jax.experimental.pallas import tpu as pltpu
from jax.sharding import PartitionSpec as P

STEPS = 8
HALO = 8
DT = 0.4
NU = 0.5


def synthesis_weights(total, shards, rows):
    omega = (np.arange(total, dtype=np.float64) + 1.0) * (math.pi / total)
    phase = np.arange(STEPS)[:, None] * omega[None, :]
    table = np.stack([np.cos(phase), -np.sin(phase)], axis=1) / math.sqrt(total)
    table = table.astype(np.float32).astype(jnp.bfloat16).astype(np.float32)
    local = total // shards
    eye = np.eye(rows, dtype=np.float32)
    out = []
    for i in range(shards):
        part = table[:, :, i * local : (i + 1) * local].reshape(STEPS, 2 * local)
        out.append(np.kron(part, eye))
    return np.stack(out).astype(jnp.bfloat16)


def analysis_weights(total, shards, rows):
    omega = (np.arange(total, dtype=np.float64) + 1.0) * (math.pi / total)
    phase = omega[:, None] * np.arange(1, STEPS + 1)[None, :]
    table = np.stack([np.cos(phase), -np.sin(phase)], axis=0) / math.sqrt(STEPS)
    table = table.astype(np.float32)
    high = table.astype(jnp.bfloat16).astype(np.float32)
    low = table - high
    local = total // shards
    eye = np.eye(rows, dtype=np.float32)
    out = []
    for i in range(shards):
        cut = slice(i * local, (i + 1) * local)
        hi = np.kron(high[:, cut].reshape(2 * local, STEPS), eye)
        lo = np.kron(low[:, cut].reshape(2 * local, STEPS), eye)
        out.append(np.concatenate([hi, hi, lo], axis=1))
    return np.stack(out).astype(jnp.bfloat16)


def lane_map(flag, rows, cols):
    lane = lax.broadcasted_iota(jnp.int32, (rows, cols), 1)
    return jnp.where(flag == 1, cols - 1 - lane, lane)


def reorder_lanes(x, flag):
    index = lane_map(flag, *x.shape)
    return jnp.take_along_axis(x, index, axis=1, mode="promise_in_bounds")


def synth_kernel(blocks, cuts, waits, order, flips, shard, x_ref, w_ref, *refs):
    rows = x_ref.shape[4] // blocks
    cols = x_ref.shape[5]
    depth = x_ref.shape[0] * x_ref.shape[1] * rows
    outs = refs[waits:]
    weights = w_ref[0]
    for pair in range(0, blocks, 2):
        cut = []
        for p in (pair, pair + 1):
            start = pl.multiple_of(order[p] * rows, rows)
            cut.append(x_ref[:, :, 0, 0, pl.ds(start, rows), :].reshape(depth, cols))
        made = jnp.dot(weights, jnp.concatenate(cut, axis=1), preferred_element_type=jnp.float32)
        for i, p in enumerate((pair, pair + 1)):
            part = reorder_lanes(made[:, i * cols : (i + 1) * cols], flips[order[p]])
            part = part.reshape(STEPS, rows, cols)
            for (low, high), out in zip(cuts, outs):
                out[:, 0, p * rows : (p + 1) * rows, :] = part[low:high]


def spread_of(group):
    return group[0], (group[1] - group[0] if len(group) > 1 else 1)


def synthesize(k, group, cuts, forcing_hat, weights, order, flips, shard, after):
    parts, local, _, _, rows, cols = forcing_hat.shape
    blocks = order.shape[0]
    first, stride = spread_of(group)
    many = len(group)
    return pl.pallas_call(
        functools.partial(synth_kernel, blocks, cuts, len(after)),
        out_shape=[jax.ShapeDtypeStruct((high - low, many, rows, cols), jnp.float32) for low, high in cuts],
        grid_spec=pltpu.PrefetchScalarGridSpec(
            num_scalar_prefetch=3,
            grid=(many,),
            in_specs=[
                pl.BlockSpec(
                    (parts, local, 1, 1, rows, cols), lambda g, *_: (0, 0, k, first + g * stride, 0, 0)
                ),
                pl.BlockSpec((1,) + weights.shape[1:], lambda g, o, f, s: (s[0], 0, 0)),
            ]
            + [pl.BlockSpec(memory_space=pl.ANY)] * len(after),
            out_specs=[pl.BlockSpec((high - low, 1, rows, cols), lambda g, *_: (0, g, 0, 0)) for low, high in cuts],
        ),
        cost_estimate=pl.CostEstimate(flops=10**9, bytes_accessed=2 * 10**6 * many, transcendentals=0),
        name=f"synth{k}_{first}",
    )(order, flips, shard, forcing_hat, weights, *after)


def chain_kernel(blocks, order, flips, speed_ref, chain_ref):
    rows = speed_ref.shape[0] // blocks
    for p in range(blocks):
        start = pl.multiple_of(order[p] * rows, rows)
        chain_ref[p * rows : (p + 1) * rows, :] = reorder_lanes(speed_ref[pl.ds(start, rows), :], flips[order[p]])


def chain_speed(speed, order, flips):
    smem = pl.BlockSpec(memory_space=pltpu.SMEM)
    vmem = pl.BlockSpec(memory_space=pltpu.VMEM)
    return pl.pallas_call(
        functools.partial(chain_kernel, order.shape[0]),
        out_shape=jax.ShapeDtypeStruct(speed.shape, speed.dtype),
        in_specs=[smem, smem, vmem],
        out_specs=vmem,
        name="chain_speed",
    )(order, flips, speed)


def total_of(terms, *index):
    own = terms[0][index]
    for term in terms[1:]:
        own = own + term[index]
    return own


def edge_kernel(sizes, *refs):
    tail_ref, head_ref = refs[-2:]
    at, field = 0, 0
    steps = STEPS - 1
    for count, many in sizes:
        terms = refs[at : at + count]
        rows = terms[0].shape[2]
        tail_ref[:, field : field + many] = total_of(
            terms, slice(0, steps), slice(None), slice(rows - HALO, rows), slice(None)
        )
        head_ref[:, field : field + many] = total_of(terms, slice(0, steps), slice(None), slice(0, HALO), slice(None))
        at, field = at + count, field + many


def edges(pieces, after):
    steps = STEPS - 1
    cols = pieces[0][0].shape[3]
    fields = sum(p[0].shape[1] for p in pieces)
    vmem = pl.BlockSpec(memory_space=pltpu.VMEM)
    flat = [t for p in pieces for t in p]
    shape = jax.ShapeDtypeStruct((steps, fields, HALO, cols), jnp.float32)
    return pl.pallas_call(
        functools.partial(edge_kernel, [(len(p), p[0].shape[1]) for p in pieces]),
        out_shape=(shape, shape),
        in_specs=[vmem] * len(flat) + [pl.BlockSpec(memory_space=pl.ANY)] * len(after),
        out_specs=(vmem, vmem),
        cost_estimate=pl.CostEstimate(flops=10**6, bytes_accessed=10**6, transcendentals=0),
        name="edges",
    )(*flat, *after)


def advance(group, window, speed, forced):
    held = {}

    def around(v):
        if v not in held:
            center, upper, lower = window(v)
            cols = center.shape[1]
            lane = lax.broadcasted_iota(jnp.int32, center.shape, 1)
            right = jnp.where(lane == cols - 1, 0.0, pltpu.roll(center, cols - 1, 1))
            left = jnp.where(lane == 0, 0.0, pltpu.roll(center, 1, 1))
            stream = 0.5 * (upper - lower)
            cross = 0.5 * (right - left)
            spread = NU * (upper + lower + right + left - 4.0 * center)
            held[v] = center, stream, cross, spread
        return held[v]

    def divergence():
        return around(1)[1] + around(2)[2]

    rates = {
        0: lambda: -divergence(),
        1: lambda: -around(3)[1],
        2: lambda: -around(3)[2],
        3: lambda: -divergence(),
        4: lambda: 0.0,
    }
    for v in group:
        center, stream, _, spread = around(v)
        yield center + DT * (rates[v]() - speed * stream + spread + forced(v))


def piece_of(group, sizes, refs, v):
    at, first = 0, 0
    where = group.index(v)
    for count, many in sizes:
        if where < first + many:
            return refs[at : at + count], where - first
        at, first = at + count, first + many


def march_kernel(group, sizes, carrier, place, *refs):
    used = sum(c for c, _ in sizes)
    terms, rest = refs[:used], refs[used:]
    before_ref, after_ref, speed_ref = rest[:3]
    other = rest[3] if carrier else None
    past_ref = rest[-1]
    rows = terms[0].shape[2]
    span = rows + 2 * HALO
    past_ref[0] = jnp.zeros(past_ref.shape[1:], jnp.float32)
    speed = speed_ref[...]
    row = lax.broadcasted_iota(jnp.int32, speed.shape, 0)
    low = jnp.where(place[0] == 0, HALO, 0)
    high = jnp.where(place[0] == place[1] - 1, span - HALO, span)
    inside = (row >= low) & (row < high)

    def step(n, carry):
        def window(v):
            if v in group:
                center = past_ref[n, group.index(v)]
            else:
                center = other[n, carrier.index(v)]
            return center, pltpu.roll(center, span - 1, 0), pltpu.roll(center, 1, 0)

        def forced(v):
            held, i = piece_of(group, sizes, terms, v)
            g = group.index(v)
            return jnp.concatenate([before_ref[n, g], total_of(held, n, i), after_ref[n, g]], axis=0)

        for g, new in enumerate(advance(group, window, speed, forced)):
            past_ref[n + 1, g] = jnp.where(inside, new, 0.0)
        return carry

    lax.fori_loop(0, STEPS - 1, step, 0)


def march(group, pieces, before, after, speed, place, carrier, other):
    _, _, rows, cols = pieces[0][0].shape
    span = rows + 2 * HALO
    vmem = pl.BlockSpec(memory_space=pltpu.VMEM)
    flat = [t for p in pieces for t in p]
    operands = [*flat, before, after, speed] + ([other] if carrier else [])
    return pl.pallas_call(
        functools.partial(march_kernel, group, [(len(p), p[0].shape[1]) for p in pieces], carrier),
        out_shape=jax.ShapeDtypeStruct((STEPS, len(group), span, cols), jnp.float32),
        in_specs=[pl.BlockSpec(memory_space=pltpu.SMEM)] + [vmem] * len(operands),
        out_specs=vmem,
        cost_estimate=pl.CostEstimate(flops=10**8, bytes_accessed=4 * 10**6, transcendentals=0),
        name="march",
    )(place, *operands)


def finish_kernel(blocks, group, sizes, carrier, order, flips, shard, past_ref, *refs):
    used = sum(c for c, _ in sizes)
    terms, rest = refs[:used], refs[used:]
    speed_ref, w_ref = rest[:2]
    other = rest[2] if carrier else None
    out_ref, last = refs[-2:]
    _, rows, cols = last.shape
    g = pl.program_id(0)

    @pl.when(g == 0)
    def _():
        def window(v):
            if v in group:
                source, i = past_ref, group.index(v)
            else:
                source, i = other, carrier.index(v)
            return tuple(source[STEPS - 1, i, pl.ds(HALO + d, rows), :] for d in (0, 1, -1))

        def forced(v):
            held, i = piece_of(group, sizes, terms, v)
            return total_of(held, held[0].shape[0] - 1, i)

        for i, new in enumerate(advance(group, window, speed_ref[HALO : HALO + rows, :], forced)):
            last[i] = new

    weights = w_ref[0]
    size = rows // blocks
    for b in range(blocks):
        where = jnp.int32(0)
        for p in range(1, blocks):
            where = jnp.where(order[p] == b, p, where)
        columns = []
        for h in range(0, size, HALO):
            start = pl.multiple_of(where * size + h, HALO)
            x = jnp.concatenate(
                [past_ref[1:, g, pl.ds(start + HALO, HALO), :], last[g, pl.ds(start, HALO), :][None]], axis=0
            ).reshape(STEPS * HALO, cols)
            x = reorder_lanes(x, flips[b])
            hi = x.astype(jnp.bfloat16)
            lo = (x - hi.astype(jnp.float32)).astype(jnp.bfloat16)
            columns.append(jnp.concatenate([hi, lo, hi], axis=0))
        made = jnp.dot(weights, jnp.concatenate(columns, axis=1), preferred_element_type=jnp.float32)
        for i, h in enumerate(range(0, size, HALO)):
            part = made[:, i * cols : (i + 1) * cols]
            part = part.reshape(out_ref.shape[0], out_ref.shape[1], HALO, cols)
            out_ref[:, :, 0, 0, b * size + h : b * size + h + HALO, :] = part


def finish(k, group, shape, past, pieces, speed, weights, order, flips, shard, carrier, other, partial):
    parts, local, _, _, rows, cols = shape
    blocks = order.shape[0]
    first, stride = spread_of(group)

    def whole(x):
        return pl.BlockSpec(x.shape, lambda g, *_: (0,) * x.ndim)

    flat = [t for p in pieces for t in p]
    operands = [order, flips, shard, past, *flat, speed, weights]
    specs = [whole(x) for x in (past, *flat, speed)]
    specs.append(pl.BlockSpec((1,) + weights.shape[1:], lambda g, o, f, s: (s[0], 0, 0)))
    if carrier:
        operands.append(other)
        specs.append(whole(other))
    aliases = {}
    if partial is not None:
        aliases = {len(operands): 0}
        operands.append(partial)
        specs.append(pl.BlockSpec(memory_space=pl.ANY))
    return pl.pallas_call(
        functools.partial(finish_kernel, blocks, group, [(len(p), p[0].shape[1]) for p in pieces], carrier),
        out_shape=jax.ShapeDtypeStruct(shape, jnp.float32),
        grid_spec=pltpu.PrefetchScalarGridSpec(
            num_scalar_prefetch=3,
            grid=(len(group),),
            in_specs=specs,
            out_specs=pl.BlockSpec(
                (parts, local, 1, 1, rows, cols), lambda g, *_: (0, 0, k, first + g * stride, 0, 0)
            ),
            scratch_shapes=[pltpu.VMEM((len(group), rows, cols), jnp.float32)],
        ),
        input_output_aliases=aliases,
        cost_estimate=pl.CostEstimate(flops=10**9, bytes_accessed=3 * 10**6 * len(group), transcendentals=0),
        name=f"finish{k}_{first}",
    )(*operands)


def shared(x):
    peers = lax.axis_size("freq")
    if peers == 2:
        return [x, lax.ppermute(x, "freq", [(0, 1), (1, 0)])]
    return [lax.psum(x, "freq")]


def neighbours(tail, head):
    peers = lax.axis_size("blk")
    up = [(i, i + 1) for i in range(peers - 1)]
    down = [(j, i) for i, j in up]
    return lax.ppermute(tail, "blk", up), lax.ppermute(head, "blk", down)


def plan(vectors):
    every, whole = (0, 1, 2, 3, 4), ((0, STEPS),)
    jobs = []
    for k in range(vectors):
        jobs.append((k, every, ((every, whole),), ()))
    return jobs


def local(forcing_hat, mean_speed, block_order, block_flips):
    peers = lax.axis_size("freq")
    total = forcing_hat.shape[1] * peers
    shape = forcing_hat.shape
    size = shape[4] // block_order.shape[0]
    shard = lax.axis_index("freq").astype(jnp.int32).reshape(1)
    place = jnp.stack([lax.axis_index("blk"), lax.axis_size("blk")]).astype(jnp.int32)
    synth = jnp.asarray(synthesis_weights(total, peers, size))
    analysis = jnp.asarray(analysis_weights(total, peers, HALO))
    jobs = plan(shape[2])
    sent, earlier = [], ()
    for k, _, parts, _ in jobs:
        pieces = []
        for part, cuts in parts:
            made = synthesize(k, part, cuts, forcing_hat, synth, block_order, block_flips, shard, earlier)
            earlier = (made[0],)
            pieces.append([shared(x) for x in made])
        sent.append(pieces)
    chain = chain_speed(mean_speed, block_order, block_flips)
    above, below = neighbours(chain[-HALO:], chain[:HALO])
    speed = jnp.concatenate([above, chain, below], axis=0)
    out = None
    history = {}
    for (k, group, _, carrier), made in zip(jobs, sent):
        early = [piece[0] for piece in made]
        late = [piece[-1] for piece in made]
        before, after = neighbours(*edges(early, () if out is None else (out,)))
        other = history.get((k, carrier))
        past = march(group, early, before, after, speed, place, carrier, other)
        history[k, group] = past
        out = finish(
            k, group, shape, past, late, speed, analysis, block_order, block_flips, shard, carrier, other, out
        )
    return out


def solution(mesh):
    placed = (P(None, "freq", None, None, "blk", None), P("blk", None), P("blk"), P("blk"))
    return jax.shard_map(
        local,
        mesh=mesh,
        in_specs=placed,
        out_specs=P(None, "freq", None, None, "blk", None),
        check_vma=False,
    )
```

```python
import functools
import math

import jax
import jax.numpy as jnp
import numpy as np
from jax import lax
from jax.experimental import pallas as pl
from jax.experimental.pallas import tpu as pltpu
from jax.sharding import PartitionSpec as P

STEPS = 8
HALO = 8
DT = 0.4
NU = 0.5


def synthesis_weights(total, shards, rows):
    omega = (np.arange(total, dtype=np.float64) + 1.0) * (math.pi / total)
    phase = np.arange(STEPS)[:, None] * omega[None, :]
    table = np.stack([np.cos(phase), -np.sin(phase)], axis=1) / math.sqrt(total)
    table = table.astype(np.float32).astype(jnp.bfloat16).astype(np.float32)
    local = total // shards
    eye = np.eye(rows, dtype=np.float32)
    out = []
    for i in range(shards):
        part = table[:, :, i * local : (i + 1) * local].reshape(STEPS, 2 * local)
        out.append(np.kron(part, eye))
    return np.stack(out).astype(jnp.bfloat16)


def analysis_weights(total, shards, rows):
    omega = (np.arange(total, dtype=np.float64) + 1.0) * (math.pi / total)
    phase = omega[:, None] * np.arange(1, STEPS + 1)[None, :]
    table = np.stack([np.cos(phase), -np.sin(phase)], axis=0) / math.sqrt(STEPS)
    table = table.astype(np.float32)
    high = table.astype(jnp.bfloat16).astype(np.float32)
    low = table - high
    local = total // shards
    eye = np.eye(rows, dtype=np.float32)
    out = []
    for i in range(shards):
        cut = slice(i * local, (i + 1) * local)
        hi = np.kron(high[:, cut].reshape(2 * local, STEPS), eye)
        lo = np.kron(low[:, cut].reshape(2 * local, STEPS), eye)
        out.append(np.concatenate([hi, hi, lo], axis=1))
    return np.stack(out).astype(jnp.bfloat16)


def lane_map(flag, rows, cols):
    lane = lax.broadcasted_iota(jnp.int32, (rows, cols), 1)
    return jnp.where(flag == 1, cols - 1 - lane, lane)


def reorder_lanes(x, flag):
    index = lane_map(flag, *x.shape)
    return jnp.take_along_axis(x, index, axis=1, mode="promise_in_bounds")


def synth_kernel(blocks, cuts, waits, order, flips, shard, x_ref, w_ref, *refs):
    rows = x_ref.shape[4] // blocks
    cols = x_ref.shape[5]
    depth = x_ref.shape[0] * x_ref.shape[1] * rows
    outs = refs[waits:]
    weights = w_ref[0]
    for pair in range(0, blocks, 2):
        cut = []
        for p in (pair, pair + 1):
            start = pl.multiple_of(order[p] * rows, rows)
            cut.append(x_ref[:, :, 0, 0, pl.ds(start, rows), :].reshape(depth, cols))
        made = jnp.dot(weights, jnp.concatenate(cut, axis=1), preferred_element_type=jnp.float32)
        for i, p in enumerate((pair, pair + 1)):
            part = reorder_lanes(made[:, i * cols : (i + 1) * cols], flips[order[p]])
            part = part.reshape(STEPS, rows, cols)
            for (low, high), out in zip(cuts, outs):
                out[:, 0, p * rows : (p + 1) * rows, :] = part[low:high]


def spread_of(group):
    return group[0], (group[1] - group[0] if len(group) > 1 else 1)


def synthesize(k, group, cuts, forcing_hat, weights, order, flips, shard, after):
    parts, local, _, _, rows, cols = forcing_hat.shape
    blocks = order.shape[0]
    first, stride = spread_of(group)
    many = len(group)
    return pl.pallas_call(
        functools.partial(synth_kernel, blocks, cuts, len(after)),
        out_shape=[jax.ShapeDtypeStruct((high - low, many, rows, cols), jnp.float32) for low, high in cuts],
        grid_spec=pltpu.PrefetchScalarGridSpec(
            num_scalar_prefetch=3,
            grid=(many,),
            in_specs=[
                pl.BlockSpec(
                    (parts, local, 1, 1, rows, cols), lambda g, *_: (0, 0, k, first + g * stride, 0, 0)
                ),
                pl.BlockSpec((1,) + weights.shape[1:], lambda g, o, f, s: (s[0], 0, 0)),
            ]
            + [pl.BlockSpec(memory_space=pl.ANY)] * len(after),
            out_specs=[pl.BlockSpec((high - low, 1, rows, cols), lambda g, *_: (0, g, 0, 0)) for low, high in cuts],
        ),
        cost_estimate=pl.CostEstimate(flops=10**9, bytes_accessed=2 * 10**6 * many, transcendentals=0),
        name=f"synth{k}_{first}",
    )(order, flips, shard, forcing_hat, weights, *after)


def chain_kernel(blocks, order, flips, speed_ref, chain_ref):
    rows = speed_ref.shape[0] // blocks
    for p in range(blocks):
        start = pl.multiple_of(order[p] * rows, rows)
        chain_ref[p * rows : (p + 1) * rows, :] = reorder_lanes(speed_ref[pl.ds(start, rows), :], flips[order[p]])


def chain_speed(speed, order, flips):
    smem = pl.BlockSpec(memory_space=pltpu.SMEM)
    vmem = pl.BlockSpec(memory_space=pltpu.VMEM)
    return pl.pallas_call(
        functools.partial(chain_kernel, order.shape[0]),
        out_shape=jax.ShapeDtypeStruct(speed.shape, speed.dtype),
        in_specs=[smem, smem, vmem],
        out_specs=vmem,
        name="chain_speed",
    )(order, flips, speed)


def total_of(terms, *index):
    own = terms[0][index]
    for term in terms[1:]:
        own = own + term[index]
    return own


def advance(group, window, speed, forced):
    held = {}

    def around(v):
        if v not in held:
            center, upper, lower = window(v)
            cols = center.shape[1]
            lane = lax.broadcasted_iota(jnp.int32, center.shape, 1)
            right = jnp.where(lane == cols - 1, 0.0, pltpu.roll(center, cols - 1, 1))
            left = jnp.where(lane == 0, 0.0, pltpu.roll(center, 1, 1))
            stream = 0.5 * (upper - lower)
            cross = 0.5 * (right - left)
            spread = NU * (upper + lower + right + left - 4.0 * center)
            held[v] = center, stream, cross, spread
        return held[v]

    def divergence():
        return around(1)[1] + around(2)[2]

    rates = {
        0: lambda: -divergence(),
        1: lambda: -around(3)[1],
        2: lambda: -around(3)[2],
        3: lambda: -divergence(),
        4: lambda: 0.0,
    }
    for v in group:
        center, stream, _, spread = around(v)
        yield center + DT * (rates[v]() - speed * stream + spread + forced(v))


def piece_of(group, sizes, refs, v):
    at, first = 0, 0
    where = group.index(v)
    for count, many in sizes:
        if where < first + many:
            return refs[at : at + count], where - first
        at, first = at + count, first + many


def march_kernel(count, waits, *refs):
    terms, speed_ref = refs[:count], refs[count]
    past_ref, span_ref, force, speeds, sent, got = refs[count + 1 + waits :]
    me, peers = lax.axis_index("blk"), lax.axis_size("blk")
    steps = STEPS - 1
    rows = terms[0].shape[2]
    span = rows + 2 * HALO
    own = pl.ds(HALO, rows)
    force[:, :, own, :] = total_of(terms, slice(0, steps))
    speeds[own, :] = speed_ref[...]
    has_before, has_after = me > 0, me < peers - 1
    after = {"blk": lax.rem(me + 1, peers)}
    before = {"blk": lax.rem(me + peers - 1, peers)}

    def move(ref, i, source, target, device):
        lead = (slice(None),) * (len(ref.shape) - 2)
        return pltpu.make_async_remote_copy(
            src_ref=ref.at[lead + (pl.ds(source, HALO), slice(None))],
            dst_ref=ref.at[lead + (pl.ds(target, HALO), slice(None))],
            send_sem=sent.at[i],
            recv_sem=got.at[i],
            device_id=device,
            device_id_type=pl.DeviceIdType.MESH,
        )

    forward = [move(force, 0, rows, 0, after), move(speeds, 1, rows, 0, after)]
    backward = [move(force, 2, HALO, HALO + rows, before), move(speeds, 3, HALO, HALO + rows, before)]
    barrier = pltpu.get_barrier_semaphore()

    @pl.when(has_after)
    def _():
        pl.semaphore_signal(barrier, inc=1, device_id=after, device_id_type=pl.DeviceIdType.MESH)

    @pl.when(has_before)
    def _():
        pl.semaphore_signal(barrier, inc=1, device_id=before, device_id_type=pl.DeviceIdType.MESH)

    inner = has_after & has_before

    @pl.when(inner)
    def _():
        pl.semaphore_wait(barrier, 2)

    @pl.when((has_after | has_before) & jnp.logical_not(inner))
    def _():
        pl.semaphore_wait(barrier, 1)

    @pl.when(has_after)
    def _():
        for copy in forward:
            copy.start()

    @pl.when(has_before)
    def _():
        for copy in backward:
            copy.start()

    @pl.when(me == 0)
    def _():
        force[:, :, 0:HALO, :] = jnp.zeros((steps, force.shape[1], HALO, force.shape[3]), jnp.float32)
        speeds[0:HALO, :] = jnp.zeros((HALO, force.shape[3]), jnp.float32)

    @pl.when(me == peers - 1)
    def _():
        force[:, :, HALO + rows :, :] = jnp.zeros((steps, force.shape[1], HALO, force.shape[3]), jnp.float32)
        speeds[HALO + rows :, :] = jnp.zeros((HALO, force.shape[3]), jnp.float32)

    past_ref[0] = jnp.zeros(past_ref.shape[1:], jnp.float32)

    @pl.when(has_after)
    def _():
        for copy in forward:
            copy.wait_send()
        for copy in backward:
            copy.wait_recv()

    @pl.when(has_before)
    def _():
        for copy in backward:
            copy.wait_send()
        for copy in forward:
            copy.wait_recv()

    speed = speeds[...]
    span_ref[...] = speed
    row = lax.broadcasted_iota(jnp.int32, speed.shape, 0)
    low = jnp.where(me == 0, HALO, 0)
    high = jnp.where(me == peers - 1, span - HALO, span)
    inside = (row >= low) & (row < high)
    fields = range(force.shape[1])

    def step(n, carry):
        def window(v):
            center = past_ref[n, v]
            return center, pltpu.roll(center, span - 1, 0), pltpu.roll(center, 1, 0)

        for v, new in enumerate(advance(fields, window, speed, lambda v: force[n, v])):
            past_ref[n + 1, v] = jnp.where(inside, new, 0.0)
        return carry

    lax.fori_loop(0, steps, step, 0)


def march(k, terms, speed, after):
    _, fields, rows, cols = terms[0].shape
    span = rows + 2 * HALO
    vmem = pl.BlockSpec(memory_space=pltpu.VMEM)
    return pl.pallas_call(
        functools.partial(march_kernel, len(terms), len(after)),
        out_shape=(
            jax.ShapeDtypeStruct((STEPS, fields, span, cols), jnp.float32),
            jax.ShapeDtypeStruct((span, cols), jnp.float32),
        ),
        in_specs=[vmem] * (len(terms) + 1) + [pl.BlockSpec(memory_space=pl.ANY)] * len(after),
        out_specs=(vmem, vmem),
        scratch_shapes=[
            pltpu.VMEM((STEPS - 1, fields, span, cols), jnp.float32),
            pltpu.VMEM((span, cols), jnp.float32),
            pltpu.SemaphoreType.DMA((4,)),
            pltpu.SemaphoreType.DMA((4,)),
        ],
        compiler_params=pltpu.CompilerParams(collective_id=k, has_side_effects=True),
        cost_estimate=pl.CostEstimate(flops=10**8, bytes_accessed=4 * 10**6, transcendentals=0),
        name=f"march{k}",
    )(*terms, speed, *after)


def finish_kernel(blocks, group, sizes, carrier, order, flips, shard, past_ref, *refs):
    used = sum(c for c, _ in sizes)
    terms, rest = refs[:used], refs[used:]
    speed_ref, w_ref = rest[:2]
    other = rest[2] if carrier else None
    out_ref, last = refs[-2:]
    _, rows, cols = last.shape
    g = pl.program_id(0)

    @pl.when(g == 0)
    def _():
        def window(v):
            if v in group:
                source, i = past_ref, group.index(v)
            else:
                source, i = other, carrier.index(v)
            return tuple(source[STEPS - 1, i, pl.ds(HALO + d, rows), :] for d in (0, 1, -1))

        def forced(v):
            held, i = piece_of(group, sizes, terms, v)
            return total_of(held, held[0].shape[0] - 1, i)

        for i, new in enumerate(advance(group, window, speed_ref[HALO : HALO + rows, :], forced)):
            last[i] = new

    weights = w_ref[0]
    size = rows // blocks
    for b in range(blocks):
        where = jnp.int32(0)
        for p in range(1, blocks):
            where = jnp.where(order[p] == b, p, where)
        columns = []
        for h in range(0, size, HALO):
            start = pl.multiple_of(where * size + h, HALO)
            x = jnp.concatenate(
                [past_ref[1:, g, pl.ds(start + HALO, HALO), :], last[g, pl.ds(start, HALO), :][None]], axis=0
            ).reshape(STEPS * HALO, cols)
            x = reorder_lanes(x, flips[b])
            hi = x.astype(jnp.bfloat16)
            lo = (x - hi.astype(jnp.float32)).astype(jnp.bfloat16)
            columns.append(jnp.concatenate([hi, lo, hi], axis=0))
        made = jnp.dot(weights, jnp.concatenate(columns, axis=1), preferred_element_type=jnp.float32)
        for i, h in enumerate(range(0, size, HALO)):
            part = made[:, i * cols : (i + 1) * cols]
            part = part.reshape(out_ref.shape[0], out_ref.shape[1], HALO, cols)
            out_ref[:, :, 0, 0, b * size + h : b * size + h + HALO, :] = part


def finish(k, group, shape, past, pieces, speed, weights, order, flips, shard, carrier, other, partial):
    parts, local, _, _, rows, cols = shape
    blocks = order.shape[0]
    first, stride = spread_of(group)

    def whole(x):
        return pl.BlockSpec(x.shape, lambda g, *_: (0,) * x.ndim)

    flat = [t for p in pieces for t in p]
    operands = [order, flips, shard, past, *flat, speed, weights]
    specs = [whole(x) for x in (past, *flat, speed)]
    specs.append(pl.BlockSpec((1,) + weights.shape[1:], lambda g, o, f, s: (s[0], 0, 0)))
    if carrier:
        operands.append(other)
        specs.append(whole(other))
    aliases = {}
    if partial is not None:
        aliases = {len(operands): 0}
        operands.append(partial)
        specs.append(pl.BlockSpec(memory_space=pl.ANY))
    return pl.pallas_call(
        functools.partial(finish_kernel, blocks, group, [(len(p), p[0].shape[1]) for p in pieces], carrier),
        out_shape=jax.ShapeDtypeStruct(shape, jnp.float32),
        grid_spec=pltpu.PrefetchScalarGridSpec(
            num_scalar_prefetch=3,
            grid=(len(group),),
            in_specs=specs,
            out_specs=pl.BlockSpec(
                (parts, local, 1, 1, rows, cols), lambda g, *_: (0, 0, k, first + g * stride, 0, 0)
            ),
            scratch_shapes=[pltpu.VMEM((len(group), rows, cols), jnp.float32)],
        ),
        input_output_aliases=aliases,
        cost_estimate=pl.CostEstimate(flops=10**9, bytes_accessed=3 * 10**6 * len(group), transcendentals=0),
        name=f"finish{k}_{first}",
    )(*operands)


def shared(x):
    peers = lax.axis_size("freq")
    if peers == 2:
        return [x, lax.ppermute(x, "freq", [(0, 1), (1, 0)])]
    return [lax.psum(x, "freq")]


def local(forcing_hat, mean_speed, block_order, block_flips):
    peers = lax.axis_size("freq")
    total = forcing_hat.shape[1] * peers
    shape = forcing_hat.shape
    size = shape[4] // block_order.shape[0]
    shard = lax.axis_index("freq").astype(jnp.int32).reshape(1)
    synth = jnp.asarray(synthesis_weights(total, peers, size))
    analysis = jnp.asarray(analysis_weights(total, peers, HALO))
    every, whole = tuple(range(shape[3])), ((0, STEPS),)
    sent, earlier = [], ()
    for k in range(shape[2]):
        made = synthesize(k, every, whole, forcing_hat, synth, block_order, block_flips, shard, earlier)
        earlier = (made[0],)
        sent.append(shared(made[0]))
    chain = chain_speed(mean_speed, block_order, block_flips)
    out = None
    for k, terms in enumerate(sent):
        past, speed = march(k, terms, chain, () if out is None else (out,))
        out = finish(
            k, every, shape, past, [terms], speed, analysis, block_order, block_flips, shard, (), None, out
        )
    return out


def solution(mesh):
    placed = (P(None, "freq", None, None, "blk", None), P("blk", None), P("blk"), P("blk"))
    return jax.shard_map(
        local,
        mesh=mesh,
        in_specs=placed,
        out_specs=P(None, "freq", None, None, "blk", None),
        check_vma=False,
    )
```

```python
import functools
import math

import jax
import jax.numpy as jnp
import numpy as np
from jax import lax
from jax.experimental import pallas as pl
from jax.experimental.pallas import tpu as pltpu
from jax.sharding import PartitionSpec as P

STEPS = 8
HALO = 8
DT = 0.4
NU = 0.5


def synthesis_weights(total, shards, rows):
    omega = (np.arange(total, dtype=np.float64) + 1.0) * (math.pi / total)
    phase = np.arange(STEPS)[:, None] * omega[None, :]
    table = np.stack([np.cos(phase), -np.sin(phase)], axis=1) / math.sqrt(total)
    table = table.astype(np.float32).astype(jnp.bfloat16).astype(np.float32)
    local = total // shards
    eye = np.eye(rows, dtype=np.float32)
    out = []
    for i in range(shards):
        part = table[:, :, i * local : (i + 1) * local].reshape(STEPS, 2 * local)
        out.append(np.kron(part, eye))
    return np.stack(out).astype(jnp.bfloat16)


def analysis_weights(total, shards, rows):
    omega = (np.arange(total, dtype=np.float64) + 1.0) * (math.pi / total)
    phase = omega[:, None] * np.arange(1, STEPS + 1)[None, :]
    table = np.stack([np.cos(phase), -np.sin(phase)], axis=0) / math.sqrt(STEPS)
    table = table.astype(np.float32)
    high = table.astype(jnp.bfloat16).astype(np.float32)
    low = table - high
    local = total // shards
    eye = np.eye(rows, dtype=np.float32)
    out = []
    for i in range(shards):
        cut = slice(i * local, (i + 1) * local)
        hi = np.kron(high[:, cut].reshape(2 * local, STEPS), eye)
        lo = np.kron(low[:, cut].reshape(2 * local, STEPS), eye)
        out.append(np.concatenate([hi, hi, lo], axis=1))
    return np.stack(out).astype(jnp.bfloat16)


def lane_map(flag, rows, cols):
    lane = lax.broadcasted_iota(jnp.int32, (rows, cols), 1)
    return jnp.where(flag == 1, cols - 1 - lane, lane)


def reorder_lanes(x, flag):
    index = lane_map(flag, *x.shape)
    return jnp.take_along_axis(x, index, axis=1, mode="promise_in_bounds")


def synth_kernel(blocks, cuts, waits, order, flips, shard, x_ref, w_ref, *refs):
    rows = x_ref.shape[4] // blocks
    cols = x_ref.shape[5]
    depth = x_ref.shape[0] * x_ref.shape[1] * rows
    outs = refs[waits:]
    weights = w_ref[0]
    for pair in range(0, blocks, 2):
        cut = []
        for p in (pair, pair + 1):
            start = pl.multiple_of(order[p] * rows, rows)
            cut.append(x_ref[:, :, 0, 0, pl.ds(start, rows), :].reshape(depth, cols))
        made = jnp.dot(weights, jnp.concatenate(cut, axis=1), preferred_element_type=jnp.float32)
        for i, p in enumerate((pair, pair + 1)):
            part = reorder_lanes(made[:, i * cols : (i + 1) * cols], flips[order[p]])
            part = part.reshape(STEPS, rows, cols)
            for (low, high), out in zip(cuts, outs):
                out[:, 0, p * rows : (p + 1) * rows, :] = part[low:high]


def spread_of(group):
    return group[0], (group[1] - group[0] if len(group) > 1 else 1)


def synthesize(k, group, cuts, forcing_hat, weights, order, flips, shard, after):
    parts, local, _, _, rows, cols = forcing_hat.shape
    blocks = order.shape[0]
    first, stride = spread_of(group)
    many = len(group)
    return pl.pallas_call(
        functools.partial(synth_kernel, blocks, cuts, len(after)),
        out_shape=[jax.ShapeDtypeStruct((high - low, many, rows, cols), jnp.float32) for low, high in cuts],
        grid_spec=pltpu.PrefetchScalarGridSpec(
            num_scalar_prefetch=3,
            grid=(many,),
            in_specs=[
                pl.BlockSpec(
                    (parts, local, 1, 1, rows, cols), lambda g, *_: (0, 0, k, first + g * stride, 0, 0)
                ),
                pl.BlockSpec((1,) + weights.shape[1:], lambda g, o, f, s: (s[0], 0, 0)),
            ]
            + [pl.BlockSpec(memory_space=pl.ANY)] * len(after),
            out_specs=[pl.BlockSpec((high - low, 1, rows, cols), lambda g, *_: (0, g, 0, 0)) for low, high in cuts],
        ),
        cost_estimate=pl.CostEstimate(flops=10**9, bytes_accessed=2 * 10**6 * many, transcendentals=0),
        name=f"synth{k}_{first}",
    )(order, flips, shard, forcing_hat, weights, *after)


def chain_kernel(blocks, order, flips, speed_ref, chain_ref):
    rows = speed_ref.shape[0] // blocks
    for p in range(blocks):
        start = pl.multiple_of(order[p] * rows, rows)
        chain_ref[p * rows : (p + 1) * rows, :] = reorder_lanes(speed_ref[pl.ds(start, rows), :], flips[order[p]])


def chain_speed(speed, order, flips):
    smem = pl.BlockSpec(memory_space=pltpu.SMEM)
    vmem = pl.BlockSpec(memory_space=pltpu.VMEM)
    return pl.pallas_call(
        functools.partial(chain_kernel, order.shape[0]),
        out_shape=jax.ShapeDtypeStruct(speed.shape, speed.dtype),
        in_specs=[smem, smem, vmem],
        out_specs=vmem,
        name="chain_speed",
    )(order, flips, speed)


def advance(group, window, speed, forced):
    held = {}

    def around(v):
        if v not in held:
            center, upper, lower = window(v)
            cols = center.shape[1]
            lane = lax.broadcasted_iota(jnp.int32, center.shape, 1)
            right = jnp.where(lane == cols - 1, 0.0, pltpu.roll(center, cols - 1, 1))
            left = jnp.where(lane == 0, 0.0, pltpu.roll(center, 1, 1))
            stream = 0.5 * (upper - lower)
            cross = 0.5 * (right - left)
            spread = NU * (upper + lower + right + left - 4.0 * center)
            held[v] = center, stream, cross, spread
        return held[v]

    def divergence():
        return around(1)[1] + around(2)[2]

    rates = {
        0: lambda: -divergence(),
        1: lambda: -around(3)[1],
        2: lambda: -around(3)[2],
        3: lambda: -divergence(),
        4: lambda: 0.0,
    }
    for v in group:
        center, stream, _, spread = around(v)
        yield center + DT * (rates[v]() - speed * stream + spread + forced(v))


def march_kernel(count, waits, *refs):
    terms, speed_ref = refs[:count], refs[count]
    past_ref, force, extra, state, speeds, sent, got, loaded = refs[count + 1 + waits :]
    me, peers = lax.axis_index("blk"), lax.axis_size("blk")
    steps = STEPS - 1
    rows = terms[0].shape[2]
    span = rows + 2 * HALO
    own = pl.ds(HALO, rows)
    has_before, has_after = me > 0, me < peers - 1
    after = {"blk": lax.rem(me + 1, peers)}
    before = {"blk": lax.rem(me + peers - 1, peers)}

    def move(ref, i, source, target, device):
        lead = (pl.ds(0, steps), slice(None))[: len(ref.shape) - 2]
        return pltpu.make_async_remote_copy(
            src_ref=ref.at[lead + (pl.ds(source, HALO), slice(None))],
            dst_ref=ref.at[lead + (pl.ds(target, HALO), slice(None))],
            send_sem=sent.at[i],
            recv_sem=got.at[i],
            device_id=device,
            device_id_type=pl.DeviceIdType.MESH,
        )

    forward = [move(force, 0, rows, 0, after), move(speeds, 1, rows, 0, after)]
    backward = [move(force, 2, HALO, HALO + rows, before), move(speeds, 3, HALO, HALO + rows, before)]
    targets = [force.at[:, :, own, :]] + [extra.at[i] for i in range(count - 1)]
    loads = [
        pltpu.make_async_copy(term, target, loaded.at[i])
        for i, (term, target) in enumerate(zip(terms, targets))
    ]
    for load in loads:
        load.start()
    barrier = pltpu.get_barrier_semaphore()

    @pl.when(has_after)
    def _():
        pl.semaphore_signal(barrier, inc=1, device_id=after, device_id_type=pl.DeviceIdType.MESH)

    @pl.when(has_before)
    def _():
        pl.semaphore_signal(barrier, inc=1, device_id=before, device_id_type=pl.DeviceIdType.MESH)

    speeds[own, :] = speed_ref[...]
    force[steps, :, 0:HALO, :] = jnp.zeros((force.shape[1], HALO, force.shape[3]), jnp.float32)
    force[steps, :, HALO + rows :, :] = jnp.zeros((force.shape[1], HALO, force.shape[3]), jnp.float32)
    state[0] = jnp.zeros(state.shape[1:], jnp.float32)
    for load in loads:
        load.wait()
    for i in range(count - 1):
        force[:, :, own, :] += extra[i]
    inner = has_after & has_before

    @pl.when(inner)
    def _():
        pl.semaphore_wait(barrier, 2)

    @pl.when((has_after | has_before) & jnp.logical_not(inner))
    def _():
        pl.semaphore_wait(barrier, 1)

    @pl.when(has_after)
    def _():
        for copy in forward:
            copy.start()

    @pl.when(has_before)
    def _():
        for copy in backward:
            copy.start()

    @pl.when(me == 0)
    def _():
        force[0:steps, :, 0:HALO, :] = jnp.zeros((steps, force.shape[1], HALO, force.shape[3]), jnp.float32)
        speeds[0:HALO, :] = jnp.zeros((HALO, force.shape[3]), jnp.float32)

    @pl.when(me == peers - 1)
    def _():
        force[0:steps, :, HALO + rows :, :] = jnp.zeros((steps, force.shape[1], HALO, force.shape[3]), jnp.float32)
        speeds[HALO + rows :, :] = jnp.zeros((HALO, force.shape[3]), jnp.float32)

    @pl.when(has_after)
    def _():
        for copy in forward:
            copy.wait_send()
        for copy in backward:
            copy.wait_recv()

    @pl.when(has_before)
    def _():
        for copy in backward:
            copy.wait_send()
        for copy in forward:
            copy.wait_recv()

    speed = speeds[...]
    row = lax.broadcasted_iota(jnp.int32, speed.shape, 0)
    low = jnp.where(me == 0, HALO, 0)
    high = jnp.where(me == peers - 1, span - HALO, span)
    inside = (row >= low) & (row < high)
    fields = range(force.shape[1])

    def step(n, carry):
        now = lax.rem(n, 2)

        def window(v):
            center = state[now, v]
            return center, pltpu.roll(center, span - 1, 0), pltpu.roll(center, 1, 0)

        for v, new in enumerate(advance(fields, window, speed, lambda v: force[n, v])):
            new = jnp.where(inside, new, 0.0)
            state[1 - now, v] = new
            past_ref[n, v] = new[HALO : HALO + rows]
        return carry

    lax.fori_loop(0, STEPS, step, 0)


def march(k, terms, speed, after):
    _, fields, rows, cols = terms[0].shape
    span = rows + 2 * HALO
    vmem = pl.BlockSpec(memory_space=pltpu.VMEM)
    anywhere = pl.BlockSpec(memory_space=pl.ANY)
    return pl.pallas_call(
        functools.partial(march_kernel, len(terms), len(after)),
        out_shape=jax.ShapeDtypeStruct((STEPS, fields, rows, cols), jnp.float32),
        in_specs=[anywhere] * len(terms) + [vmem] + [anywhere] * len(after),
        out_specs=vmem,
        scratch_shapes=[
            pltpu.VMEM((STEPS, fields, span, cols), jnp.float32),
            pltpu.VMEM((max(len(terms) - 1, 1), STEPS, fields, rows, cols), jnp.float32),
            pltpu.VMEM((2, fields, span, cols), jnp.float32),
            pltpu.VMEM((span, cols), jnp.float32),
            pltpu.SemaphoreType.DMA((4,)),
            pltpu.SemaphoreType.DMA((4,)),
            pltpu.SemaphoreType.DMA((len(terms),)),
        ],
        compiler_params=pltpu.CompilerParams(collective_id=k, has_side_effects=True, vmem_limit_bytes=16 << 20),
        cost_estimate=pl.CostEstimate(flops=10**8, bytes_accessed=4 * 10**6, transcendentals=0),
        name=f"march{k}",
    )(*terms, speed, *after)


def finish_kernel(blocks, order, flips, shard, past_ref, w_ref, *refs):
    out_ref = refs[-1]
    rows, cols = past_ref.shape[2:]
    weights = w_ref[0]
    size = rows // blocks
    for b in range(blocks):
        where = jnp.int32(0)
        for p in range(1, blocks):
            where = jnp.where(order[p] == b, p, where)
        columns = []
        for h in range(0, size, HALO):
            start = pl.multiple_of(where * size + h, HALO)
            x = past_ref[:, 0, pl.ds(start, HALO), :].reshape(STEPS * HALO, cols)
            x = reorder_lanes(x, flips[b])
            hi = x.astype(jnp.bfloat16)
            lo = (x - hi.astype(jnp.float32)).astype(jnp.bfloat16)
            columns.append(jnp.concatenate([hi, lo, hi], axis=0))
        made = jnp.dot(weights, jnp.concatenate(columns, axis=1), preferred_element_type=jnp.float32)
        for i, h in enumerate(range(0, size, HALO)):
            part = made[:, i * cols : (i + 1) * cols]
            part = part.reshape(out_ref.shape[0], out_ref.shape[1], HALO, cols)
            out_ref[:, :, 0, 0, b * size + h : b * size + h + HALO, :] = part


def finish(k, shape, past, weights, order, flips, shard, partial):
    parts, local, _, fields, rows, cols = shape
    blocks = order.shape[0]
    operands = [order, flips, shard, past, weights]
    specs = [
        pl.BlockSpec((STEPS, 1, rows, cols), lambda v, *_: (0, v, 0, 0)),
        pl.BlockSpec((1,) + weights.shape[1:], lambda v, o, f, s: (s[0], 0, 0)),
    ]
    aliases = {}
    if partial is not None:
        aliases = {len(operands): 0}
        operands.append(partial)
        specs.append(pl.BlockSpec(memory_space=pl.ANY))
    return pl.pallas_call(
        functools.partial(finish_kernel, blocks),
        out_shape=jax.ShapeDtypeStruct(shape, jnp.float32),
        grid_spec=pltpu.PrefetchScalarGridSpec(
            num_scalar_prefetch=3,
            grid=(fields,),
            in_specs=specs,
            out_specs=pl.BlockSpec((parts, local, 1, 1, rows, cols), lambda v, *_: (0, 0, k, v, 0, 0)),
        ),
        input_output_aliases=aliases,
        cost_estimate=pl.CostEstimate(flops=10**9, bytes_accessed=12 * 10**6, transcendentals=0),
        name=f"finish{k}",
    )(*operands)


def shared(x):
    peers = lax.axis_size("freq")
    if peers == 2:
        return [x, lax.ppermute(x, "freq", [(0, 1), (1, 0)])]
    return [lax.psum(x, "freq")]


def local(forcing_hat, mean_speed, block_order, block_flips):
    peers = lax.axis_size("freq")
    total = forcing_hat.shape[1] * peers
    shape = forcing_hat.shape
    size = shape[4] // block_order.shape[0]
    shard = lax.axis_index("freq").astype(jnp.int32).reshape(1)
    synth = jnp.asarray(synthesis_weights(total, peers, size))
    analysis = jnp.asarray(analysis_weights(total, peers, HALO))
    every, whole = tuple(range(shape[3])), ((0, STEPS),)
    sent, earlier = [], ()
    for k in range(shape[2]):
        made = synthesize(k, every, whole, forcing_hat, synth, block_order, block_flips, shard, earlier)
        earlier = (made[0],)
        sent.append(shared(made[0]))
    chain = chain_speed(mean_speed, block_order, block_flips)
    out = None
    for k, terms in enumerate(sent):
        past = march(k, terms, chain, () if out is None else (out,))
        out = finish(k, shape, past, analysis, block_order, block_flips, shard, out)
    return out


def solution(mesh):
    placed = (P(None, "freq", None, None, "blk", None), P("blk", None), P("blk"), P("blk"))
    return jax.shard_map(
        local,
        mesh=mesh,
        in_specs=placed,
        out_specs=P(None, "freq", None, None, "blk", None),
        check_vma=False,
    )
```

```python
import functools
import math

import jax
import jax.numpy as jnp
import numpy as np
from jax import lax
from jax.experimental import pallas as pl
from jax.experimental.pallas import tpu as pltpu
from jax.sharding import PartitionSpec as P

STEPS = 8
HALO = 8
DT = 0.4
NU = 0.5


def synthesis_weights(total, shards, rows):
    omega = (np.arange(total, dtype=np.float64) + 1.0) * (math.pi / total)
    phase = np.arange(STEPS)[:, None] * omega[None, :]
    table = np.stack([np.cos(phase), -np.sin(phase)], axis=1) / math.sqrt(total)
    table = table.astype(np.float32).astype(jnp.bfloat16).astype(np.float32)
    local = total // shards
    eye = np.eye(rows, dtype=np.float32)
    out = []
    for i in range(shards):
        part = table[:, :, i * local : (i + 1) * local].reshape(STEPS, 2 * local)
        out.append(np.kron(part, eye))
    return np.stack(out).astype(jnp.bfloat16)


def analysis_weights(total, shards, rows):
    omega = (np.arange(total, dtype=np.float64) + 1.0) * (math.pi / total)
    phase = omega[:, None] * np.arange(1, STEPS + 1)[None, :]
    table = np.stack([np.cos(phase), -np.sin(phase)], axis=0) / math.sqrt(STEPS)
    table = table.astype(np.float32)
    high = table.astype(jnp.bfloat16).astype(np.float32)
    low = table - high
    local = total // shards
    eye = np.eye(rows, dtype=np.float32)
    out = []
    for i in range(shards):
        cut = slice(i * local, (i + 1) * local)
        hi = np.kron(high[:, cut].reshape(2 * local, STEPS), eye)
        lo = np.kron(low[:, cut].reshape(2 * local, STEPS), eye)
        out.append(np.concatenate([hi, hi, lo], axis=1))
    return np.stack(out).astype(jnp.bfloat16)


def lane_map(flag, rows, cols):
    lane = lax.broadcasted_iota(jnp.int32, (rows, cols), 1)
    return jnp.where(flag == 1, cols - 1 - lane, lane)


def reorder_lanes(x, flag):
    index = lane_map(flag, *x.shape)
    return jnp.take_along_axis(x, index, axis=1, mode="promise_in_bounds")


def synth_kernel(blocks, cuts, waits, order, flips, shard, x_ref, w_ref, *refs):
    rows = x_ref.shape[4] // blocks
    cols = x_ref.shape[5]
    depth = x_ref.shape[0] * x_ref.shape[1] * rows
    outs = refs[waits:]
    weights = w_ref[0]
    for pair in range(0, blocks, 2):
        cut = []
        for p in (pair, pair + 1):
            start = pl.multiple_of(order[p] * rows, rows)
            cut.append(x_ref[:, :, 0, 0, pl.ds(start, rows), :].reshape(depth, cols))
        made = jnp.dot(weights, jnp.concatenate(cut, axis=1), preferred_element_type=jnp.float32)
        for i, p in enumerate((pair, pair + 1)):
            part = reorder_lanes(made[:, i * cols : (i + 1) * cols], flips[order[p]])
            part = part.reshape(STEPS, rows, cols)
            for (low, high), out in zip(cuts, outs):
                out[:, 0, p * rows : (p + 1) * rows, :] = part[low:high]


def spread_of(group):
    return group[0], (group[1] - group[0] if len(group) > 1 else 1)


def synthesize(k, group, cuts, forcing_hat, weights, order, flips, shard, after):
    parts, local, _, _, rows, cols = forcing_hat.shape
    blocks = order.shape[0]
    first, stride = spread_of(group)
    many = len(group)
    return pl.pallas_call(
        functools.partial(synth_kernel, blocks, cuts, len(after)),
        out_shape=[jax.ShapeDtypeStruct((high - low, many, rows, cols), jnp.float32) for low, high in cuts],
        grid_spec=pltpu.PrefetchScalarGridSpec(
            num_scalar_prefetch=3,
            grid=(many,),
            in_specs=[
                pl.BlockSpec(
                    (parts, local, 1, 1, rows, cols), lambda g, *_: (0, 0, k, first + g * stride, 0, 0)
                ),
                pl.BlockSpec((1,) + weights.shape[1:], lambda g, o, f, s: (s[0], 0, 0)),
            ]
            + [pl.BlockSpec(memory_space=pl.ANY)] * len(after),
            out_specs=[pl.BlockSpec((high - low, 1, rows, cols), lambda g, *_: (0, g, 0, 0)) for low, high in cuts],
        ),
        cost_estimate=pl.CostEstimate(flops=10**9, bytes_accessed=2 * 10**6 * many, transcendentals=0),
        name=f"synth{k}_{first}",
    )(order, flips, shard, forcing_hat, weights, *after)


def chain_kernel(blocks, order, flips, speed_ref, chain_ref):
    rows = speed_ref.shape[0] // blocks
    for p in range(blocks):
        start = pl.multiple_of(order[p] * rows, rows)
        chain_ref[p * rows : (p + 1) * rows, :] = reorder_lanes(speed_ref[pl.ds(start, rows), :], flips[order[p]])


def chain_speed(speed, order, flips):
    smem = pl.BlockSpec(memory_space=pltpu.SMEM)
    vmem = pl.BlockSpec(memory_space=pltpu.VMEM)
    return pl.pallas_call(
        functools.partial(chain_kernel, order.shape[0]),
        out_shape=jax.ShapeDtypeStruct(speed.shape, speed.dtype),
        in_specs=[smem, smem, vmem],
        out_specs=vmem,
        name="chain_speed",
    )(order, flips, speed)


def advance(group, window, speed, forced):
    held = {}

    def around(v):
        if v not in held:
            center, upper, lower = window(v)
            cols = center.shape[1]
            lane = lax.broadcasted_iota(jnp.int32, center.shape, 1)
            right = jnp.where(lane == cols - 1, 0.0, pltpu.roll(center, cols - 1, 1))
            left = jnp.where(lane == 0, 0.0, pltpu.roll(center, 1, 1))
            stream = 0.5 * (upper - lower)
            cross = 0.5 * (right - left)
            spread = NU * (upper + lower + right + left - 4.0 * center)
            held[v] = center, stream, cross, spread
        return held[v]

    def divergence():
        return around(1)[1] + around(2)[2]

    rates = {
        0: lambda: -divergence(),
        1: lambda: -around(3)[1],
        2: lambda: -around(3)[2],
        3: lambda: -divergence(),
        4: lambda: 0.0,
    }
    for v in group:
        center, stream, _, spread = around(v)
        yield center + DT * (rates[v]() - speed * stream + spread + forced(v))


def march_kernel(count, waits, *refs):
    terms, speed_ref = refs[:count], refs[count]
    past_ref, force, extra, state, speeds, sent, got, loaded = refs[count + 1 + waits :]
    me, peers = lax.axis_index("blk"), lax.axis_size("blk")
    steps = STEPS - 1
    rows = terms[0].shape[2]
    span = rows + 2 * HALO
    own = pl.ds(HALO, rows)
    has_before, has_after = me > 0, me < peers - 1
    after = {"blk": lax.rem(me + 1, peers)}
    before = {"blk": lax.rem(me + peers - 1, peers)}

    def move(ref, i, source, target, device):
        lead = (pl.ds(0, steps), slice(None))[: len(ref.shape) - 2]
        return pltpu.make_async_remote_copy(
            src_ref=ref.at[lead + (pl.ds(source, HALO), slice(None))],
            dst_ref=ref.at[lead + (pl.ds(target, HALO), slice(None))],
            send_sem=sent.at[i],
            recv_sem=got.at[i],
            device_id=device,
            device_id_type=pl.DeviceIdType.MESH,
        )

    forward = [move(force, 0, rows, 0, after), move(speeds, 1, rows, 0, after)]
    backward = [move(force, 2, HALO, HALO + rows, before), move(speeds, 3, HALO, HALO + rows, before)]
    targets = [force.at[:, :, own, :]] + [extra.at[i] for i in range(count - 1)]
    loads = [
        pltpu.make_async_copy(term, target, loaded.at[i])
        for i, (term, target) in enumerate(zip(terms, targets))
    ]
    for load in loads:
        load.start()
    barrier = pltpu.get_barrier_semaphore()

    @pl.when(has_after)
    def _():
        pl.semaphore_signal(barrier, inc=1, device_id=after, device_id_type=pl.DeviceIdType.MESH)

    @pl.when(has_before)
    def _():
        pl.semaphore_signal(barrier, inc=1, device_id=before, device_id_type=pl.DeviceIdType.MESH)

    speeds[own, :] = speed_ref[...]
    force[steps, :, 0:HALO, :] = jnp.zeros((force.shape[1], HALO, force.shape[3]), jnp.float32)
    force[steps, :, HALO + rows :, :] = jnp.zeros((force.shape[1], HALO, force.shape[3]), jnp.float32)
    state[0] = jnp.zeros(state.shape[1:], jnp.float32)
    for load in loads:
        load.wait()
    for i in range(count - 1):
        force[:, :, own, :] += extra[i]
    inner = has_after & has_before

    @pl.when(inner)
    def _():
        pl.semaphore_wait(barrier, 2)

    @pl.when((has_after | has_before) & jnp.logical_not(inner))
    def _():
        pl.semaphore_wait(barrier, 1)

    @pl.when(has_after)
    def _():
        for copy in forward:
            copy.start()

    @pl.when(has_before)
    def _():
        for copy in backward:
            copy.start()

    @pl.when(me == 0)
    def _():
        force[0:steps, :, 0:HALO, :] = jnp.zeros((steps, force.shape[1], HALO, force.shape[3]), jnp.float32)
        speeds[0:HALO, :] = jnp.zeros((HALO, force.shape[3]), jnp.float32)

    @pl.when(me == peers - 1)
    def _():
        force[0:steps, :, HALO + rows :, :] = jnp.zeros((steps, force.shape[1], HALO, force.shape[3]), jnp.float32)
        speeds[HALO + rows :, :] = jnp.zeros((HALO, force.shape[3]), jnp.float32)

    @pl.when(has_after)
    def _():
        for copy in forward:
            copy.wait_send()
        for copy in backward:
            copy.wait_recv()

    @pl.when(has_before)
    def _():
        for copy in backward:
            copy.wait_send()
        for copy in forward:
            copy.wait_recv()

    speed = speeds[...]
    row = lax.broadcasted_iota(jnp.int32, speed.shape, 0)
    low = jnp.where(me == 0, HALO, 0)
    high = jnp.where(me == peers - 1, span - HALO, span)
    inside = (row >= low) & (row < high)
    fields = range(force.shape[1])

    def step(n, carry):
        now = lax.rem(n, 2)

        def window(v):
            center = state[now, v]
            return center, pltpu.roll(center, span - 1, 0), pltpu.roll(center, 1, 0)

        for v, new in enumerate(advance(fields, window, speed, lambda v: force[n, v])):
            new = jnp.where(inside, new, 0.0)
            state[1 - now, v] = new
            past_ref[n, v] = new[HALO : HALO + rows]
        return carry

    lax.fori_loop(0, STEPS, step, 0)


def march(k, terms, speed, after):
    _, fields, rows, cols = terms[0].shape
    span = rows + 2 * HALO
    vmem = pl.BlockSpec(memory_space=pltpu.VMEM)
    anywhere = pl.BlockSpec(memory_space=pl.ANY)
    return pl.pallas_call(
        functools.partial(march_kernel, len(terms), len(after)),
        out_shape=jax.ShapeDtypeStruct((STEPS, fields, rows, cols), jnp.float32),
        in_specs=[anywhere] * len(terms) + [vmem] + [anywhere] * len(after),
        out_specs=vmem,
        scratch_shapes=[
            pltpu.VMEM((STEPS, fields, span, cols), jnp.float32),
            pltpu.VMEM((max(len(terms) - 1, 1), STEPS, fields, rows, cols), jnp.float32),
            pltpu.VMEM((2, fields, span, cols), jnp.float32),
            pltpu.VMEM((span, cols), jnp.float32),
            pltpu.SemaphoreType.DMA((4,)),
            pltpu.SemaphoreType.DMA((4,)),
            pltpu.SemaphoreType.DMA((len(terms),)),
        ],
        compiler_params=pltpu.CompilerParams(collective_id=k, has_side_effects=True, vmem_limit_bytes=16 << 20),
        cost_estimate=pl.CostEstimate(flops=10**8, bytes_accessed=4 * 10**6, transcendentals=0),
        name=f"march{k}",
    )(*terms, speed, *after)


def finish_kernel(blocks, order, flips, shard, past_ref, w_ref, *refs):
    out_ref, token_ref = refs[-2:]
    rows, cols = past_ref.shape[2:]
    token_ref[...] = jnp.zeros_like(token_ref)
    weights = w_ref[0]
    size = rows // blocks
    for b in range(blocks):
        where = jnp.int32(0)
        for p in range(1, blocks):
            where = jnp.where(order[p] == b, p, where)
        columns = []
        for h in range(0, size, HALO):
            start = pl.multiple_of(where * size + h, HALO)
            x = past_ref[:, 0, pl.ds(start, HALO), :].reshape(STEPS * HALO, cols)
            x = reorder_lanes(x, flips[b])
            hi = x.astype(jnp.bfloat16)
            lo = (x - hi.astype(jnp.float32)).astype(jnp.bfloat16)
            columns.append(jnp.concatenate([hi, lo, hi], axis=0))
        made = jnp.dot(weights, jnp.concatenate(columns, axis=1), preferred_element_type=jnp.float32)
        for i, h in enumerate(range(0, size, HALO)):
            part = made[:, i * cols : (i + 1) * cols]
            part = part.reshape(out_ref.shape[0], out_ref.shape[1], HALO, cols)
            out_ref[:, :, 0, 0, b * size + h : b * size + h + HALO, :] = part


def finish(k, shape, past, weights, order, flips, shard, partial):
    parts, local, _, fields, rows, cols = shape
    blocks = order.shape[0]
    operands = [order, flips, shard, past, weights]
    specs = [
        pl.BlockSpec((STEPS, 1, rows, cols), lambda v, *_: (0, v, 0, 0)),
        pl.BlockSpec((1,) + weights.shape[1:], lambda v, o, f, s: (s[0], 0, 0)),
    ]
    aliases = {}
    if partial is not None:
        aliases = {len(operands): 0}
        operands.append(partial)
        specs.append(pl.BlockSpec(memory_space=pl.ANY))
    return pl.pallas_call(
        functools.partial(finish_kernel, blocks),
        out_shape=(jax.ShapeDtypeStruct(shape, jnp.float32), jax.ShapeDtypeStruct((HALO, cols), jnp.float32)),
        grid_spec=pltpu.PrefetchScalarGridSpec(
            num_scalar_prefetch=3,
            grid=(fields,),
            in_specs=specs,
            out_specs=(
                pl.BlockSpec((parts, local, 1, 1, rows, cols), lambda v, *_: (0, 0, k, v, 0, 0)),
                pl.BlockSpec((HALO, cols), lambda v, *_: (0, 0)),
            ),
        ),
        input_output_aliases=aliases,
        cost_estimate=pl.CostEstimate(flops=10**9, bytes_accessed=12 * 10**6, transcendentals=0),
        name=f"finish{k}",
    )(*operands)


def shared(x):
    peers = lax.axis_size("freq")
    if peers == 2:
        return [x, lax.ppermute(x, "freq", [(0, 1), (1, 0)])]
    return [lax.psum(x, "freq")]


def local(forcing_hat, mean_speed, block_order, block_flips):
    peers = lax.axis_size("freq")
    total = forcing_hat.shape[1] * peers
    shape = forcing_hat.shape
    size = shape[4] // block_order.shape[0]
    shard = lax.axis_index("freq").astype(jnp.int32).reshape(1)
    synth = jnp.asarray(synthesis_weights(total, peers, size))
    analysis = jnp.asarray(analysis_weights(total, peers, HALO))
    every, whole = tuple(range(shape[3])), ((0, STEPS),)
    sent, earlier = [], ()
    for k in range(shape[2]):
        made = synthesize(k, every, whole, forcing_hat, synth, block_order, block_flips, shard, earlier)
        earlier = (made[0],)
        sent.append(shared(made[0]))
    chain = chain_speed(mean_speed, block_order, block_flips)
    out, token = None, ()
    for k, terms in enumerate(sent):
        past = march(k, terms, chain, token)
        out, *token = finish(k, shape, past, analysis, block_order, block_flips, shard, out)
    return out


def solution(mesh):
    placed = (P(None, "freq", None, None, "blk", None), P("blk", None), P("blk"), P("blk"))
    return jax.shard_map(
        local,
        mesh=mesh,
        in_specs=placed,
        out_specs=P(None, "freq", None, None, "blk", None),
        check_vma=False,
    )
```
